512 devices in a mesh: section: 2 (over core), row: 32 (over y, x), col: 8 (over z).
Axes of the slice: x: 4, y: 8, z: 8, core: 2. Of those that a mesh axis runs over, the one named last changes fastest.
Arguments:
- prior_root: float32 [512, 8, 8, 256], P(None, None, 'col'), may hold values from -0.08 to 4, as said below
- observations: float32 [2, 4096, 8, 8, 256], P('section', 'row', None, 'col'), may hold values from -0.5 to 0.5
- live_rows: int32 [2, 32], P('section', 'row'), may hold values from 1 to 128, 2560 in all within a row
Outputs:
- r_slab: float32 [2, 512, 8, 8, 256], P('section', 'row', None, 'col')
The draws below stay inside these ranges and needn't reach their ends.
Inputs may be any that keep to these rules, and one draw needn't show every extreme that they name: `prior_root`: zero where the global column is below the row, positive on the diagonal. `live_rows`: within one arc group the counts sum to 2560; the largest count of each arc group is 128.
All inputs are finite; a program needn't handle non-finite values.
Results may differ from the reference program's by a relative error of at most 0.0001.
Values sent between devices are 32-bit elements; how exact they have to be, the bound alone decides.
A program may use at most 128 MiB of HBM per device.

```python
import math
import jax
import jax.numpy as jnp
import numpy as np
from jax import lax

PANEL = 256
OBS_DEV = 128
RROWS = 512
CYC = 8
OBSROWS = 4096
GROUPS = 2
N_ROW = 32
N_COL = 8


def draw_prior_root(key, part):
    key_diag, key_upper = jax.random.split(key)
    full_shape = (RROWS, CYC, N_COL, PANEL)
    cycle_ids = jnp.arange(CYC, dtype=jnp.int32)[None, :, None, None]
    device_ids = jnp.arange(N_COL, dtype=jnp.int32)[None, None, :, None]
    within_ids = jnp.arange(PANEL, dtype=jnp.int32)[None, None, None, :]
    column_ids = (cycle_ids * N_COL + device_ids) * PANEL + within_ids
    row_ids = jnp.arange(RROWS, dtype=jnp.int32)[:, None, None, None]
    diagonal = jax.random.uniform(key_diag, full_shape, jnp.float32, 1.0, 2.0)
    upper_part = 0.02 * jax.random.truncated_normal(key_upper, -4.0, 4.0, full_shape, jnp.float32)
    zeros_part = jnp.zeros(full_shape, jnp.float32)
    values = jnp.where(column_ids == row_ids, diagonal, jnp.where(column_ids > row_ids, upper_part, zeros_part))
    return values.astype(jnp.float32)


def block_scale(rng, dims, pieces, least, largest):
    level, own = 1.0, jax.random.fold_in(rng, 6)
    for position, parts in pieces:
        heights = jnp.exp(jax.random.uniform(jax.random.fold_in(own, position), (parts,), jnp.float32, least / len(pieces), largest / len(pieces)))
        level = level * jnp.repeat(heights, dims[position] // parts).reshape([-1 if axis == position else 1 for axis in range(len(dims))])
    return level


def split_up(number_of, total, limit, slope):
    portions = [(1 << 20) // math.isqrt(rank ** slope) + 1 for rank in range(2, number_of + 1)]
    surplus, given = total - limit - (number_of - 1), [1] * (number_of - 1)
    while surplus > 0:
        candidates = [i for i in range(number_of - 1) if given[i] < limit]
        pool, remaining = sum([portions[i] for i in candidates]), surplus
        for i in candidates:
            addition = min(limit - given[i], max(1, remaining * portions[i] // pool), surplus)
            given[i] = given[i] + addition
            surplus = surplus - addition
    return np.array([limit] + given)


def ragged(stream_key, amount, total, bound, slope):
    if amount == 2:
        one = jax.random.randint(stream_key, (), max(1, total - bound), min(bound, total - 1) + 1)
        return jnp.stack([one, total - one])
    sizes = jnp.asarray(split_up(amount, total, bound, slope), jnp.int32)
    pairs = (amount - 1) // 2
    giver, receiver = sizes[1:1 + 2 * pairs:2], sizes[2:2 + 2 * pairs:2]
    margin = jnp.minimum(giver - 1, bound - receiver)
    shifted = jax.random.randint(jax.random.fold_in(stream_key, 1), (pairs,), 0, 1 << 20) % (margin + 1)
    sizes = sizes.at[1:1 + 2 * pairs:2].set(giver - shifted).at[2:2 + 2 * pairs:2].set(receiver + shifted)
    return sizes[jax.random.permutation(jax.random.fold_in(stream_key, 2), amount)]


def noise(rng, dims, spread, most, cuts=(), kind=jnp.bfloat16):
    array = spread * jax.random.normal(rng, dims, jnp.float32)
    if cuts:
        array = array * block_scale(rng, dims, cuts, -0.22, 0.18)
    return jnp.clip(array, -most, most).astype(kind)


def setup_inputs(seed: int = 0) -> dict:
    key_of = jax.random.split(jax.random.key(seed), 4)
    return {
        "prior_root": draw_prior_root(jax.random.fold_in(key_of[3], 71), 0),
        "observations": noise(key_of[1], (GROUPS, OBSROWS, CYC, N_COL, PANEL), OBS_DEV ** -0.5, 0.5, ((0, 2), (1, 32), (3, 8)), jnp.float32),
        "live_rows": jax.vmap(lambda own: ragged(own, N_ROW, OBSROWS * 5 // 8, OBS_DEV, 2))(jax.random.split(key_of[2], GROUPS)).reshape((GROUPS, N_ROW)).astype(jnp.int32),
    }


def gram_product(left, right):
    return lax.dot_general(left.astype(jnp.float32), right.astype(jnp.float32), (((0,), (0,)), ((), ())), precision=lax.Precision.HIGHEST, preferred_element_type=jnp.float32)

def reference(prior_root, observations, live_rows):
    width = CYC * N_COL * PANEL
    prior_rows = prior_root.reshape(RROWS, width)
    column_ids = jnp.arange(width, dtype=jnp.int32)
    row_ids = jnp.arange(RROWS, dtype=jnp.int32)
    slot_ids = jnp.arange(OBS_DEV, dtype=jnp.int32)
    results = []
    for group in range(GROUPS):
        observed = observations[group].reshape(OBSROWS, width)
        live_mask = (slot_ids[None, :] < live_rows[group][:, None]).reshape(OBSROWS)
        observed = jnp.where(live_mask[:, None], observed, jnp.zeros_like(observed))
        information = gram_product(prior_rows[:, :RROWS], prior_rows) + gram_product(observed[:, :RROWS], observed)
        lower_factor = jnp.linalg.cholesky(information[:, :RROWS])
        slab_rows = lax.linalg.triangular_solve(lower_factor, information, left_side=True, lower=True)
        slab_rows = jnp.where(column_ids[None, :] >= row_ids[:, None], slab_rows, jnp.zeros_like(slab_rows))
        results.append(slab_rows)
        prior_rows = slab_rows
    return jnp.stack(results).reshape(GROUPS, RROWS, CYC, N_COL, PANEL)
```

```python
import functools

import jax
import jax.numpy as jnp
from jax import lax
from jax.experimental import pallas as pl
from jax.experimental.pallas import tpu as pltpu
from jax.sharding import PartitionSpec as P

F32 = jnp.float32
NX, NY, NZ, NS = 4, 8, 8, 2
NR = NX * NY
OBS = 128
PRI = 16
ROWS = OBS + PRI
CHUNKS = 3
CH = ROWS // CHUNKS
MESH = pl.DeviceIdType.MESH


def dot(a, b, ca, cb):
    return lax.dot_general(
        a, b, (((ca,), (cb,)), ((), ())), precision=lax.Precision.HIGHEST, preferred_element_type=F32
    )


def rcopy(src, dst, send, recv, device):
    return pltpu.make_async_remote_copy(
        src_ref=src, dst_ref=dst, send_sem=send, recv_sem=recv, device_id=device, device_id_type=MESH
    )


def inverse_factor(rows):
    groups, n = len(rows), rows[0].shape[1]
    lane = lax.broadcasted_iota(jnp.int32, (8, n), 1)
    sub = lax.broadcasted_iota(jnp.int32, (8, n), 0)
    left = list(rows)
    right = [jnp.where(lane == sub + 8 * g, 1.0, 0.0).astype(F32) for g in range(groups)]
    for m in range(groups):
        cols = {
            g: [jnp.broadcast_to(left[g][:, 8 * m + j : 8 * m + j + 1], (8, n)) for j in range(8)]
            for g in range(m, groups)
        }
        pivot = {
            (i, j): jnp.broadcast_to(cols[m][j][i : i + 1, :], (8, n)) for j in range(8) for i in range(j, 8)
        }
        top_left = [jnp.broadcast_to(left[m][j : j + 1, :], (8, n)) for j in range(8)]
        top_right = [jnp.broadcast_to(right[m][j : j + 1, :], (8, n)) for j in range(8)]
        for j in range(8):
            scale = lax.rsqrt(pivot[j, j])
            top_left[j] = top_left[j] * scale
            top_right[j] = top_right[j] * scale
            for i in range(j + 1, 8):
                pivot[i, j] = pivot[i, j] * scale
            for g in range(m + 1, groups):
                cols[g][j] = cols[g][j] * scale
            for k in range(j + 1, 8):
                factor = pivot[k, j]
                for i in range(k, 8):
                    pivot[i, k] = pivot[i, k] - pivot[i, j] * factor
                top_left[k] = top_left[k] - top_left[j] * factor
                top_right[k] = top_right[k] - top_right[j] * factor
                for g in range(m + 1, groups):
                    cols[g][k] = cols[g][k] - cols[g][j] * factor
        for g in range(m + 1, groups):
            from_left, from_right = cols[g][0] * top_left[0], cols[g][0] * top_right[0]
            for j in range(1, 8):
                from_left = from_left + cols[g][j] * top_left[j]
                from_right = from_right + cols[g][j] * top_right[j]
            left[g] = left[g] - from_left
            right[g] = right[g] - from_right
        done = top_right[0]
        for j in range(1, 8):
            done = jnp.where(sub == j, top_right[j], done)
        right[m] = done
    return right


def gather_kernel(
    live, obs_hbm, prior_hbm, info, shares,
    obs, prior, xv, xo, pan, dpart, dgot, dsum, dother, bt, bgot, bother,
    lsem, zs, zr, xos, xor_, xps, xpr, d1s, d1r, ss, sr, d2s, d2r, ys, yr,
):
    s, r, c = lax.axis_index("section"), lax.axis_index("row"), lax.axis_index("col")
    y, x = r // NX, r % NX
    other = (1 - s, r, c)

    load_obs = pltpu.make_async_copy(obs_hbm, obs, lsem.at[0])
    load_obs.start()
    load_prior = pltpu.make_async_copy(prior_hbm.at[pl.ds(r * PRI, PRI)], prior, lsem.at[1])
    load_prior.start()

    def plane(offset):
        q = (c * NX + x + offset) % (NX * NZ)
        return (s, y * NX + q % NX, q // NX), q

    barrier = pltpu.get_barrier_semaphore()

    def greet(offset, carry):
        pl.semaphore_signal(barrier, inc=1, device_id=plane(offset)[0], device_id_type=MESH)
        return carry

    lax.fori_loop(1, NX * NZ, greet, 0)
    for o in range(1, NY):
        pl.semaphore_signal(barrier, inc=1, device_id=(s, (y + o) % NY * NX + x, c), device_id_type=MESH)
    pl.semaphore_signal(barrier, inc=1, device_id=other, device_id_type=MESH)

    alive = lax.broadcasted_iota(jnp.int32, (OBS, 128), 0) < live[0, 0]
    first = jnp.full((PRI, 128), s, jnp.int32) == 0
    load_obs.wait()
    load_prior.wait()

    def part(l):
        return jnp.where(alive, obs[:, l, :], 0.0), jnp.where(first, prior[:, l, :], 0.0)

    base = pl.multiple_of(x * ROWS, 8)
    for l in range(2):
        top, bottom = part(l)
        xv[0:OBS, 128 * l : 128 * l + 128] = top
        xv[OBS:ROWS, 128 * l : 128 * l + 128] = bottom
    for h in range(2):

        @pl.when(c == h)
        def _():
            pan[pl.ds(base, ROWS), 256 * h : 256 * h + 256] = xv[:, 0:256]

    pl.semaphore_wait(barrier, NX * NZ - 1 + NY - 1 + 1)

    def piece(h, i, xs):
        start = pl.multiple_of(xs * ROWS + i * CH, 8)
        return pan.at[pl.ds(start, CH), 256 * h : 256 * h + 256]

    below = jnp.where(c == 0, NZ - 1, jnp.where(c <= NZ // 2, c + 1, c - 1))
    ends = (c == NZ // 2) | (c == NZ // 2 + 1)

    def down(h, i):
        return rcopy(piece(h, i, x), piece(h, i, x), zs.at[h, i], zr.at[h, i], (s, r, below))

    def cross(h, i):
        return rcopy(piece(h, i, x), piece(h, i, x), zs.at[h + 2, i], zr.at[h, i], (s, r, 1 - h))

    def side(h, i, o):
        return rcopy(
            piece(h, i, x), piece(h, i, x), xps.at[o - 1, h, i], xpr.at[x, h, i],
            (s, y * NX + (x + o) % NX, c),
        )

    for i in range(CHUNKS):
        for h in range(2):

            @pl.when(c == h)
            def _():
                cross(h, i).start()
                down(h, i).start()

    for l in range(2, 16):
        top, bottom = part(l)
        xv[0:OBS, 128 * l : 128 * l + 128] = top
        xv[OBS:ROWS, 128 * l : 128 * l + 128] = bottom

    def across(o):
        xt = (x + o) % NX
        return rcopy(
            xv.at[:, pl.ds(pl.multiple_of(xt * 512, 128), 512)], xo.at[pl.ds(base, ROWS), :],
            xos.at[o - 1], xor_.at[x], (s, y * NX + xt, c),
        )

    for o in range(1, NX):
        across(o).start()
    xo[pl.ds(base, ROWS), :] = xv[:, pl.ds(pl.multiple_of(x * 512, 128), 512)]

    for i in range(CHUNKS):
        for h in range(2):

            @pl.when(c != h)
            def _():
                down(h, i).wait_recv()

                @pl.when(jnp.logical_not(ends))
                def _():
                    down(h, i).start()

            for o in range(1, NX):
                side(h, i, o).start()

    def from_side(h, i, o):
        xs = (x + o) % NX
        return rcopy(
            piece(h, i, xs), piece(h, i, xs), xps.at[o - 1, h, i], xpr.at[xs, h, i], (s, y * NX + xs, c)
        )

    for i in range(CHUNKS):
        for h in range(2):
            for o in range(1, NX):
                from_side(h, i, o).wait_recv()

    xlane = pl.multiple_of(x * 128, 128)
    for k in range(4):
        dpart[k] = dot(pan[:, 128 * k : 128 * k + 128], pan[:, pl.ds(xlane, 128)], 0, 0)
    crow = pl.multiple_of(c * 16, 8)

    def d1(o):
        yt = (y + o) % NY
        return rcopy(dpart.at[:, pl.ds(crow, 16), :], dgot.at[y], d1s.at[o - 1], d1r.at[y], (s, yt * NX + x, c))

    def d1_from(o):
        ys_ = (y + o) % NY
        return rcopy(dpart.at[:, pl.ds(crow, 16), :], dgot.at[ys_], d1s.at[o - 1], d1r.at[ys_], (s, ys_ * NX + x, c))

    for o in range(1, NY):
        d1(o).start()
    dgot[y] = dpart[:, pl.ds(crow, 16), :]

    for o in range(1, NX):
        xs = (x + o) % NX
        rcopy(
            xv.at[:, pl.ds(pl.multiple_of(x * 512, 128), 512)],
            xo.at[pl.ds(pl.multiple_of(xs * ROWS, 8), ROWS), :],
            xos.at[o - 1], xor_.at[xs], (s, y * NX + xs, c),
        ).wait_recv()

    for t in range(2):
        bt[2 * t] = dot(xo[:, 128 * 2 * t : 128 * 2 * t + 128], pan[...], 0, 0)
        bt[2 * t + 1] = dot(xo[:, 128 * 2 * t + 128 : 128 * 2 * t + 256], pan[...], 0, 0)

    def yslice(yt):
        return bt.at[yt // 2, pl.ds(pl.multiple_of(yt % 2 * 64, 8), 64), :]

    def y1(o):
        yt = (y + o) % NY
        return rcopy(yslice(yt), bgot.at[y], ys.at[o - 1], yr.at[y], (s, yt * NX + x, c))

    def y1_from(o):
        yf = (y + o) % NY
        return rcopy(yslice(yf), bgot.at[yf], ys.at[o - 1], yr.at[yf], (s, yf * NX + x, c))

    for o in range(1, NY):
        y1(o).start()
    bgot[y] = bt[y // 2, pl.ds(pl.multiple_of(y % 2 * 64, 8), 64), :]

    for o in range(1, NY):
        d1_from(o).wait_recv()
    total = dgot[0]
    for o in range(1, NY):
        total = total + dgot[o]
    dsum[...] = total
    swap_d = rcopy(dsum, dother, ss.at[0], sr.at[0], other)
    swap_d.start()
    swap_d.wait()
    second = jnp.full((4, 16, 128), s, jnp.int32) == 1
    dsum[...] = dsum[...] + jnp.where(second, dother[...], 0.0)
    info[:, pl.ds(crow, 16), pl.ds(xlane, 128)] = dsum[...]

    def place(q):
        return info.at[:, pl.ds(pl.multiple_of(q // NX * 16, 8), 16), pl.ds(pl.multiple_of(q % NX * 128, 128), 128)]

    me = c * NX + x

    def d2(o):
        device, q = plane(o)
        return rcopy(dsum, place(me), d2s.at[o], d2r.at[me], device)

    def d2_from(o):
        device, q = plane(o)
        return rcopy(dsum, place(q), d2s.at[o], d2r.at[q], device)

    def begin(o, carry):
        d2(o).start()
        return carry

    def finish(o, carry):
        d2_from(o).wait_recv()
        d2(o).wait_send()
        return carry

    lax.fori_loop(1, NX * NZ, begin, 0)

    for o in range(1, NY):
        y1_from(o).wait_recv()
    both = bgot[0]
    for o in range(1, NY):
        both = both + bgot[o]
    shares[...] = both
    swap_b = rcopy(shares, bother, ss.at[1], sr.at[1], other)
    swap_b.start()
    swap_b.wait()
    second = jnp.full((64, 512), s, jnp.int32) == 1
    shares[...] = shares[...] + jnp.where(second, bother[...], 0.0)

    lax.fori_loop(1, NX * NZ, finish, 0)

    for i in range(CHUNKS):
        for h in range(2):

            @pl.when(c == h)
            def _():
                cross(h, i).wait_send()

            @pl.when((c == h) | jnp.logical_not(ends))
            def _():
                down(h, i).wait_send()

            for o in range(1, NX):
                side(h, i, o).wait_send()
    for o in range(1, NX):
        across(o).wait_send()
    for o in range(1, NY):
        d1(o).wait_send()
        y1(o).wait_send()


def factor_kernel(info, shares, out, a, bt, linv, w):
    a[...] = info[...]
    bt[...] = shares[...]

    def panel(k, carry):
        start = pl.multiple_of(k * 128, 128)
        rows = [a[k, 8 * g : 8 * g + 8, pl.ds(start, 128)] for g in range(16)]
        right = inverse_factor(rows)
        for g in range(16):
            linv[8 * g : 8 * g + 8, :] = right[g]
        w[...] = dot(linv[...], a[k], 1, 0)
        solved = dot(linv[...], bt[:, pl.ds(start, 128)], 1, 1)
        out[pl.ds(start, 128), :] = solved
        bt[...] = bt[...] - dot(solved, w[...], 0, 0)
        for i in range(1, 4):
            a[i] = a[i] - dot(w[:, 128 * i : 128 * i + 128], w[...], 0, 0)
        return carry

    lax.fori_loop(0, 4, panel, 0)


def spread_kernel(solved, out, got, sends, recvs):
    s, r, c = lax.axis_index("section"), lax.axis_index("row"), lax.axis_index("col")
    barrier = pltpu.get_barrier_semaphore()

    def greet(o, carry):
        pl.semaphore_signal(barrier, inc=1, device_id=(s, (r + o) % NR, c), device_id_type=MESH)
        return carry

    lax.fori_loop(1, NR, greet, 0)
    pl.semaphore_wait(barrier, NR - 1)

    def rows_of(q):
        return solved.at[pl.ds(pl.multiple_of(q * 16, 8), 16), :]

    def push(o):
        q = (r + o) % NR
        return rcopy(rows_of(q), got.at[r], sends.at[o], recvs.at[r], (s, q, c))

    def pull(o):
        q = (r + o) % NR
        return rcopy(rows_of(q), got.at[q], sends.at[o], recvs.at[q], (s, q, c))

    def begin(o, carry):
        push(o).start()
        return carry

    def finish(o, carry):
        pull(o).wait_recv()
        push(o).wait_send()
        return carry

    lax.fori_loop(1, NR, begin, 0)
    got[r] = solved[pl.ds(pl.multiple_of(r * 16, 8), 16), :]
    lax.fori_loop(1, NR, finish, 0)
    row_ids = r * 16 + lax.broadcasted_iota(jnp.int32, (16, 128), 0)
    lanes = lax.broadcasted_iota(jnp.int32, (16, 128), 1)
    for l in range(16):
        cyc, half = l // 2, l % 2
        xs, y0 = cyc // 2, cyc % 2 * 4 + half * 2
        both = jnp.concatenate([got[y0 * NX + xs], got[(y0 + 1) * NX + xs]], axis=1)
        column_ids = (cyc * NZ + c) * 256 + half * 128 + lanes
        out[:, l, :] = jnp.where(column_ids >= row_ids, both, 0.0)


def on_device(prior_root, observations, live_rows):
    vmem = pl.BlockSpec(memory_space=pltpu.VMEM)
    anywhere = pl.BlockSpec(memory_space=pl.ANY)
    dma = pltpu.SemaphoreType.DMA
    info, shares = pl.pallas_call(
        gather_kernel,
        out_shape=(jax.ShapeDtypeStruct((4, 128, 512), F32), jax.ShapeDtypeStruct((64, 512), F32)),
        in_specs=[pl.BlockSpec(memory_space=pltpu.SMEM), anywhere, anywhere],
        out_specs=(vmem, vmem),
        scratch_shapes=[
            pltpu.VMEM((OBS, 16, 128), F32),
            pltpu.VMEM((PRI, 16, 128), F32),
            pltpu.VMEM((ROWS, 2048), F32),
            pltpu.VMEM((NX * ROWS, 512), F32),
            pltpu.VMEM((NX * ROWS, 512), F32),
            pltpu.VMEM((4, 128, 128), F32),
            pltpu.VMEM((NY, 4, 16, 128), F32),
            pltpu.VMEM((4, 16, 128), F32),
            pltpu.VMEM((4, 16, 128), F32),
            pltpu.VMEM((4, 128, 512), F32),
            pltpu.VMEM((NY, 64, 512), F32),
            pltpu.VMEM((64, 512), F32),
            dma((2,)),
            dma((4, CHUNKS)),
            dma((2, CHUNKS)),
            dma((NX - 1,)),
            dma((NX,)),
            dma((NX - 1, 2, CHUNKS)),
            dma((NX, 2, CHUNKS)),
            dma((NY - 1,)),
            dma((NY,)),
            dma((2,)),
            dma((2,)),
            dma((NX * NZ,)),
            dma((NX * NZ,)),
            dma((NY - 1,)),
            dma((NY,)),
        ],
        compiler_params=pltpu.CompilerParams(
            collective_id=0, has_side_effects=True, vmem_limit_bytes=40 << 20
        ),
        name="gather",
    )(live_rows, observations.reshape(OBS, 16, 128), prior_root.reshape(512, 16, 128))
    solved = pl.pallas_call(
        factor_kernel,
        out_shape=jax.ShapeDtypeStruct((512, 64), F32),
        in_specs=[vmem, vmem],
        out_specs=vmem,
        scratch_shapes=[
            pltpu.VMEM((4, 128, 512), F32),
            pltpu.VMEM((64, 512), F32),
            pltpu.VMEM((128, 128), F32),
            pltpu.VMEM((128, 512), F32),
        ],
        name="factor",
    )(info, shares)
    rows = pl.pallas_call(
        spread_kernel,
        out_shape=jax.ShapeDtypeStruct((16, 16, 128), F32),
        in_specs=[vmem],
        out_specs=vmem,
        scratch_shapes=[pltpu.VMEM((NR, 16, 64), F32), dma((NR,)), dma((NR,))],
        compiler_params=pltpu.CompilerParams(collective_id=1, has_side_effects=True),
        name="spread",
    )(solved)
    return rows.reshape(1, 16, 8, 1, 256)


def solution(mesh):
    placed = (
        P(None, None, "col", None),
        P("section", "row", None, "col", None),
        P("section", "row"),
    )
    return jax.shard_map(
        on_device,
        mesh=mesh,
        in_specs=placed,
        out_specs=P("section", "row", None, "col", None),
        check_vma=False,
    )
```

```python
import functools

import jax
import jax.numpy as jnp
from jax import lax
from jax.experimental import pallas as pl
from jax.experimental.pallas import tpu as pltpu
from jax.sharding import PartitionSpec as P

F32 = jnp.float32
NX, NY, NZ, NS = 4, 8, 8, 2
NR = NX * NY
OBS = 128
PRI = 16
ROWS = OBS + PRI
CHUNKS = 3
CH = ROWS // CHUNKS
MESH = pl.DeviceIdType.MESH


def dot(a, b, ca, cb):
    return lax.dot_general(
        a, b, (((ca,), (cb,)), ((), ())), precision=lax.Precision.HIGHEST, preferred_element_type=F32
    )


def rcopy(src, dst, send, recv, device):
    return pltpu.make_async_remote_copy(
        src_ref=src, dst_ref=dst, send_sem=send, recv_sem=recv, device_id=device, device_id_type=MESH
    )


def inverse_factor(rows):
    groups, n = len(rows), rows[0].shape[1]
    lane = lax.broadcasted_iota(jnp.int32, (8, n), 1)
    sub = lax.broadcasted_iota(jnp.int32, (8, n), 0)
    left = list(rows)
    right = [jnp.where(lane == sub + 8 * g, 1.0, 0.0).astype(F32) for g in range(groups)]
    for m in range(groups):
        cols = {
            g: [jnp.broadcast_to(left[g][:, 8 * m + j : 8 * m + j + 1], (8, n)) for j in range(8)]
            for g in range(m, groups)
        }
        pivot = {
            (i, j): jnp.broadcast_to(cols[m][j][i : i + 1, :], (8, n)) for j in range(8) for i in range(j, 8)
        }
        top_left = [jnp.broadcast_to(left[m][j : j + 1, :], (8, n)) for j in range(8)]
        top_right = [jnp.broadcast_to(right[m][j : j + 1, :], (8, n)) for j in range(8)]
        for j in range(8):
            scale = lax.rsqrt(pivot[j, j])
            top_left[j] = top_left[j] * scale
            top_right[j] = top_right[j] * scale
            for i in range(j + 1, 8):
                pivot[i, j] = pivot[i, j] * scale
            for g in range(m + 1, groups):
                cols[g][j] = cols[g][j] * scale
            for k in range(j + 1, 8):
                factor = pivot[k, j]
                for i in range(k, 8):
                    pivot[i, k] = pivot[i, k] - pivot[i, j] * factor
                top_left[k] = top_left[k] - top_left[j] * factor
                top_right[k] = top_right[k] - top_right[j] * factor
                for g in range(m + 1, groups):
                    cols[g][k] = cols[g][k] - cols[g][j] * factor
        for g in range(m + 1, groups):
            from_left, from_right = cols[g][0] * top_left[0], cols[g][0] * top_right[0]
            for j in range(1, 8):
                from_left = from_left + cols[g][j] * top_left[j]
                from_right = from_right + cols[g][j] * top_right[j]
            left[g] = left[g] - from_left
            right[g] = right[g] - from_right
        done = top_right[0]
        for j in range(1, 8):
            done = jnp.where(sub == j, top_right[j], done)
        right[m] = done
    return right


def update_kernel(
    live, obs_hbm, prior_hbm, got,
    obs, prior, xv, xo, pan, dpart, dgot, dsum, dother, info, bt, bgot, shares, bother, a, linv, w, solved,
    lsem, zs, zr, xos, xor_, xps, xpr, d1s, d1r, ss, sr, dzs, dzr, dxs, dxr, ys, yr, rs, rr,
):
    s, r, c = lax.axis_index("section"), lax.axis_index("row"), lax.axis_index("col")
    y, x = r // NX, r % NX
    other = (1 - s, r, c)

    def on_x(o):
        xt = (x + o) % NX
        return (s, y * NX + xt, c), xt

    def on_y(o):
        yt = (y + o) % NY
        return (s, yt * NX + x, c), yt

    def on_z(o):
        zt = (c + o) % NZ
        return (s, r, zt), zt

    load_obs = pltpu.make_async_copy(obs_hbm, obs, lsem.at[0])
    load_obs.start()
    load_prior = pltpu.make_async_copy(prior_hbm.at[pl.ds(r * PRI, PRI)], prior, lsem.at[1])
    load_prior.start()

    barrier = pltpu.get_barrier_semaphore()
    peers = [on_z(o)[0] for o in range(1, NZ)] + [on_x(o)[0] for o in range(1, NX)]
    peers += [on_y(o)[0] for o in range(1, NY)] + [other]
    for peer in peers:
        pl.semaphore_signal(barrier, inc=1, device_id=peer, device_id_type=MESH)

    alive = lax.broadcasted_iota(jnp.int32, (OBS, 128), 0) < live[0, 0]
    first = jnp.full((PRI, 128), s, jnp.int32) == 0
    load_obs.wait()
    load_prior.wait()
    for l in range(16):
        xv[0:OBS, 128 * l : 128 * l + 128] = jnp.where(alive, obs[:, l, :], 0.0)
        xv[OBS:ROWS, 128 * l : 128 * l + 128] = jnp.where(first, prior[:, l, :], 0.0)
    base = pl.multiple_of(x * ROWS, 8)
    for h in range(2):

        @pl.when(c == h)
        def _():
            pan[pl.ds(base, ROWS), 256 * h : 256 * h + 256] = xv[:, 0:256]

    pl.semaphore_wait(barrier, len(peers))

    def piece(h, i, xs):
        start = pl.multiple_of(xs * ROWS + i * CH, 8)
        return pan.at[pl.ds(start, CH), 256 * h : 256 * h + 256]

    below = jnp.where(c == 0, NZ - 1, jnp.where(c <= NZ // 2, c + 1, c - 1))
    ends = (c == NZ // 2) | (c == NZ // 2 + 1)

    def down(h, i):
        return rcopy(piece(h, i, x), piece(h, i, x), zs.at[h, i], zr.at[h, i], (s, r, below))

    def cross(h, i):
        return rcopy(piece(h, i, x), piece(h, i, x), zs.at[h + 2, i], zr.at[h, i], (s, r, 1 - h))

    def side(h, i, o):
        device, xt = on_x(o)
        return rcopy(piece(h, i, x), piece(h, i, x), xps.at[o - 1, h, i], xpr.at[x, h, i], device)

    def from_side(h, i, o):
        device, xs = on_x(o)
        return rcopy(piece(h, i, xs), piece(h, i, xs), xps.at[o - 1, h, i], xpr.at[xs, h, i], device)

    for i in range(CHUNKS):
        for h in range(2):

            @pl.when(c == h)
            def _():
                down(h, i).start()
                cross(h, i).start()

    for i in range(CHUNKS):
        for h in range(2):

            @pl.when(c != h)
            def _():
                down(h, i).wait_recv()

                @pl.when(jnp.logical_not(ends))
                def _():
                    down(h, i).start()

            for o in range(1, NX):
                side(h, i, o).start()

    mine = pl.multiple_of(x * 512, 128)

    def across(o):
        device, xt = on_x(o)
        columns = pl.ds(pl.multiple_of(xt * 512, 128), 512)
        return rcopy(xv.at[:, columns], xo.at[pl.ds(base, ROWS), :], xos.at[o - 1], xor_.at[x], device)

    def from_across(o):
        device, xs = on_x(o)
        rows = pl.ds(pl.multiple_of(xs * ROWS, 8), ROWS)
        return rcopy(xv.at[:, pl.ds(mine, 512)], xo.at[rows, :], xos.at[o - 1], xor_.at[xs], device)

    for o in range(1, NX):
        across(o).start()
    xo[pl.ds(base, ROWS), :] = xv[:, pl.ds(mine, 512)]

    for i in range(CHUNKS):
        for h in range(2):
            for o in range(1, NX):
                from_side(h, i, o).wait_recv()

    xlane = pl.multiple_of(x * 128, 128)
    crow = pl.multiple_of(c * 16, 8)
    for k in range(4):
        dpart[k] = dot(pan[:, 128 * k : 128 * k + 128], pan[:, pl.ds(xlane, 128)], 0, 0)

    def d1(o):
        device, yt = on_y(o)
        return rcopy(dpart.at[:, pl.ds(crow, 16), :], dgot.at[y], d1s.at[o - 1], d1r.at[y], device)

    def from_d1(o):
        device, yf = on_y(o)
        return rcopy(dpart.at[:, pl.ds(crow, 16), :], dgot.at[yf], d1s.at[o - 1], d1r.at[yf], device)

    for o in range(1, NY):
        d1(o).start()
    dgot[y] = dpart[:, pl.ds(crow, 16), :]
    for o in range(1, NY):
        from_d1(o).wait_recv()
    total = dgot[0]
    for o in range(1, NY):
        total = total + dgot[o]
    dsum[...] = total
    swap_d = rcopy(dsum, dother, ss.at[0], sr.at[0], other)
    swap_d.start()
    swap_d.wait()
    second = jnp.full((4, 16, 128), s, jnp.int32) == 1
    dsum[...] = dsum[...] + jnp.where(second, dother[...], 0.0)
    info[:, pl.ds(crow, 16), pl.ds(xlane, 128)] = dsum[...]

    blocks = (pl.ds(0, 1), pl.ds(1, 3))

    def dz(b, o):
        device, zt = on_z(o)
        return rcopy(
            dsum.at[blocks[b]], info.at[blocks[b], pl.ds(crow, 16), pl.ds(xlane, 128)],
            dzs.at[b, o - 1], dzr.at[b, c], device,
        )

    def from_dz(b, o):
        device, zf = on_z(o)
        rows = pl.ds(pl.multiple_of(zf * 16, 8), 16)
        return rcopy(
            dsum.at[blocks[b]], info.at[blocks[b], rows, pl.ds(xlane, 128)],
            dzs.at[b, o - 1], dzr.at[b, zf], device,
        )

    def dx(b, o):
        device, xt = on_x(o)
        place = info.at[blocks[b], :, pl.ds(xlane, 128)]
        return rcopy(place, place, dxs.at[b, o - 1], dxr.at[b, x], device)

    def from_dx(b, o):
        device, xf = on_x(o)
        place = info.at[blocks[b], :, pl.ds(pl.multiple_of(xf * 128, 128), 128)]
        return rcopy(place, place, dxs.at[b, o - 1], dxr.at[b, xf], device)

    for b in range(2):
        for o in range(1, NZ):
            dz(b, o).start()
    for b in range(2):
        for o in range(1, NZ):
            from_dz(b, o).wait_recv()
        for o in range(1, NX):
            dx(b, o).start()

    for o in range(1, NX):
        from_across(o).wait_recv()
    for t in range(4):
        bt[t] = dot(xo[:, 128 * t : 128 * t + 128], pan[...], 0, 0)

    def of_y(yt):
        return bt.at[yt // 2, pl.ds(pl.multiple_of(yt % 2 * 64, 8), 64), :]

    def b1(o):
        device, yt = on_y(o)
        return rcopy(of_y(yt), bgot.at[y], ys.at[o - 1], yr.at[y], device)

    def from_b1(o):
        device, yf = on_y(o)
        return rcopy(of_y(yf), bgot.at[yf], ys.at[o - 1], yr.at[yf], device)

    for o in range(1, NY):
        b1(o).start()
    bgot[y] = bt[y // 2, pl.ds(pl.multiple_of(y % 2 * 64, 8), 64), :]

    def push(q):
        rows = solved.at[pl.ds(pl.multiple_of(q * 16, 8), 16), :]
        return rcopy(rows, got.at[r], rs.at[q], rr.at[r], (s, q, c))

    def pull(q):
        rows = solved.at[pl.ds(pl.multiple_of(q * 16, 8), 16), :]
        return rcopy(rows, got.at[q], rs.at[q], rr.at[q], (s, q, c))

    def solve(k):
        start = pl.multiple_of(k * 128, 128)
        solved[pl.ds(start, 128), :] = dot(linv[k], shares[:, pl.ds(start, 128)], 1, 1)

        def send(i, carry):
            q = k * 8 + i

            @pl.when(q != r)
            def _():
                push(q).start()

            @pl.when(q == r)
            def _():
                got[r] = solved[pl.ds(pl.multiple_of(r * 16, 8), 16), :]

            return carry

        lax.fori_loop(0, 8, send, 0)

    def eliminate(k):
        start = pl.multiple_of(k * 128, 128)
        shares[...] = shares[...] - dot(solved[pl.ds(start, 128), :], w[k], 0, 0)

    for o in range(1, NX):
        from_dx(0, o).wait_recv()
    a[0] = info[0]

    def panel(k, carry):
        start = pl.multiple_of(k * 128, 128)
        rows = [a[k, 8 * g : 8 * g + 8, pl.ds(start, 128)] for g in range(16)]
        right = inverse_factor(rows)
        for g in range(16):
            linv[k, 8 * g : 8 * g + 8, :] = right[g]

        @pl.when(k == 0)
        def _():
            for o in range(1, NX):
                from_dx(1, o).wait_recv()
            a[1:4] = info[1:4]

        @pl.when(k < 3)
        def _():
            w[k] = dot(linv[k], a[k], 1, 0)
            for i in range(1, 4):
                a[i] = a[i] - dot(w[k, :, 128 * i : 128 * i + 128], w[k], 0, 0)

        @pl.when(k == 2)
        def _():
            for o in range(1, NY):
                from_b1(o).wait_recv()
            both = bgot[0]
            for o in range(1, NY):
                both = both + bgot[o]
            shares[...] = both
            swap_b = rcopy(shares, bother, ss.at[1], sr.at[1], other)
            swap_b.start()
            swap_b.wait()
            later = jnp.full((64, 512), s, jnp.int32) == 1
            shares[...] = shares[...] + jnp.where(later, bother[...], 0.0)
            for j in range(3):
                solve(j)
                eliminate(j)

        return carry

    lax.fori_loop(0, 4, panel, 0)
    solve(3)

    for i in range(CHUNKS):
        for h in range(2):

            @pl.when(c == h)
            def _():
                cross(h, i).wait_send()

            @pl.when((c == h) | jnp.logical_not(ends))
            def _():
                down(h, i).wait_send()

            for o in range(1, NX):
                side(h, i, o).wait_send()
    for o in range(1, NX):
        across(o).wait_send()
        dx(0, o).wait_send()
        dx(1, o).wait_send()
    for o in range(1, NY):
        d1(o).wait_send()
        b1(o).wait_send()
    for o in range(1, NZ):
        dz(0, o).wait_send()
        dz(1, o).wait_send()

    def finish(o, carry):
        q = (r + o) % NR
        pull(q).wait_recv()
        push(q).wait_send()
        return carry

    lax.fori_loop(1, NR, finish, 0)


def assemble_kernel(got, out):
    r, c = lax.axis_index("row"), lax.axis_index("col")
    row_ids = r * 16 + lax.broadcasted_iota(jnp.int32, (16, 128), 0)
    lanes = lax.broadcasted_iota(jnp.int32, (16, 128), 1)
    for l in range(16):
        cyc, half = l // 2, l % 2
        xs, y0 = cyc // 2, cyc % 2 * 4 + half * 2
        both = jnp.concatenate([got[y0 * NX + xs], got[(y0 + 1) * NX + xs]], axis=1)
        column_ids = (cyc * NZ + c) * 256 + half * 128 + lanes
        out[:, l, :] = jnp.where(column_ids >= row_ids, both, 0.0)


def on_device(prior_root, observations, live_rows):
    vmem = pl.BlockSpec(memory_space=pltpu.VMEM)
    hbm = pl.BlockSpec(memory_space=pltpu.HBM)

    def buf(*shape):
        return pltpu.VMEM(shape, F32)

    def dma(*shape):
        return pltpu.SemaphoreType.DMA(shape)

    got = pl.pallas_call(
        update_kernel,
        out_shape=jax.ShapeDtypeStruct((NR, 16, 64), F32),
        in_specs=[pl.BlockSpec(memory_space=pltpu.SMEM), hbm, hbm],
        out_specs=vmem,
        scratch_shapes=[
            buf(OBS, 16, 128), buf(PRI, 16, 128), buf(ROWS, 2048), buf(NX * ROWS, 512), buf(NX * ROWS, 512),
            buf(4, 128, 128), buf(NY, 4, 16, 128), buf(4, 16, 128), buf(4, 16, 128), buf(4, 128, 512),
            buf(4, 128, 512), buf(NY, 64, 512), buf(64, 512), buf(64, 512),
            buf(4, 128, 512), buf(4, 128, 128), buf(4, 128, 512), buf(512, 64),
            dma(2), dma(4, CHUNKS), dma(2, CHUNKS), dma(NX - 1), dma(NX),
            dma(NX - 1, 2, CHUNKS), dma(NX, 2, CHUNKS), dma(NY - 1), dma(NY), dma(2), dma(2),
            dma(2, NZ - 1), dma(2, NZ), dma(2, NX - 1), dma(2, NX), dma(NY - 1), dma(NY), dma(NR), dma(NR),
        ],
        compiler_params=pltpu.CompilerParams(
            collective_id=0, has_side_effects=True, vmem_limit_bytes=40 << 20
        ),
        name="update",
    )(live_rows, observations.reshape(OBS, 16, 128), prior_root.reshape(512, 16, 128))
    rows = pl.pallas_call(
        assemble_kernel,
        out_shape=jax.ShapeDtypeStruct((16, 16, 128), F32),
        in_specs=[vmem],
        out_specs=vmem,
        name="assemble",
    )(got)
    return rows.reshape(1, 16, 8, 1, 256)


def solution(mesh):
    placed = (
        P(None, None, "col", None),
        P("section", "row", None, "col", None),
        P("section", "row"),
    )
    return jax.shard_map(
        on_device,
        mesh=mesh,
        in_specs=placed,
        out_specs=P("section", "row", None, "col", None),
        check_vma=False,
    )
```

```python
import functools

import jax
import jax.numpy as jnp
from jax import lax
from jax.experimental import pallas as pl
from jax.experimental.pallas import tpu as pltpu
from jax.sharding import PartitionSpec as P

F32 = jnp.float32
NX, NY, NZ, NS = 4, 8, 8, 2
NR = NX * NY
OBS = 128
PRI = 16
ROWS = OBS + PRI
CHUNKS = 3
CH = ROWS // CHUNKS
MESH = pl.DeviceIdType.MESH


def dot(a, b, ca, cb):
    return lax.dot_general(
        a, b, (((ca,), (cb,)), ((), ())), precision=lax.Precision.HIGHEST, preferred_element_type=F32
    )


def rcopy(src, dst, send, recv, device):
    return pltpu.make_async_remote_copy(
        src_ref=src, dst_ref=dst, send_sem=send, recv_sem=recv, device_id=device, device_id_type=MESH
    )


def inverse_factor(rows):
    groups, n = len(rows), rows[0].shape[1]
    lane = lax.broadcasted_iota(jnp.int32, (8, n), 1)
    sub = lax.broadcasted_iota(jnp.int32, (8, n), 0)
    left = list(rows)
    right = [jnp.where(lane == sub + 8 * g, 1.0, 0.0).astype(F32) for g in range(groups)]
    for m in range(groups):
        cols = {
            g: [jnp.broadcast_to(left[g][:, 8 * m + j : 8 * m + j + 1], (8, n)) for j in range(8)]
            for g in range(m, groups)
        }
        pivot = {
            (i, j): jnp.broadcast_to(cols[m][j][i : i + 1, :], (8, n)) for j in range(8) for i in range(j, 8)
        }
        top_left = [jnp.broadcast_to(left[m][j : j + 1, :], (8, n)) for j in range(8)]
        top_right = [jnp.broadcast_to(right[m][j : j + 1, :], (8, n)) for j in range(8)]
        for j in range(8):
            scale = lax.rsqrt(pivot[j, j])
            top_left[j] = top_left[j] * scale
            top_right[j] = top_right[j] * scale
            for i in range(j + 1, 8):
                pivot[i, j] = pivot[i, j] * scale
            for g in range(m + 1, groups):
                cols[g][j] = cols[g][j] * scale
            for k in range(j + 1, 8):
                factor = pivot[k, j]
                for i in range(k, 8):
                    pivot[i, k] = pivot[i, k] - pivot[i, j] * factor
                top_left[k] = top_left[k] - top_left[j] * factor
                top_right[k] = top_right[k] - top_right[j] * factor
                for g in range(m + 1, groups):
                    cols[g][k] = cols[g][k] - cols[g][j] * factor
        for g in range(m + 1, groups):
            from_left, from_right = cols[g][0] * top_left[0], cols[g][0] * top_right[0]
            for j in range(1, 8):
                from_left = from_left + cols[g][j] * top_left[j]
                from_right = from_right + cols[g][j] * top_right[j]
            left[g] = left[g] - from_left
            right[g] = right[g] - from_right
        done = top_right[0]
        for j in range(1, 8):
            done = jnp.where(sub == j, top_right[j], done)
        right[m] = done
    return right


def update_kernel(
    live, obs_hbm, prior_hbm, got,
    obs, obs_lead, prior, xv, xo, pan, dfull, xgot, dpart, dgot, dsum, dother, info,
    bt, bgot, shares, bother, a, linv, w, solved,
    lsem, zs, zr, xos, xor_, xps, xpr, d0s, d0r, d1s, d1r, ss, sr, dzs, dzr, dxs, dxr, ys, yr, rs, rr,
):
    s, r, c = lax.axis_index("section"), lax.axis_index("row"), lax.axis_index("col")
    y, x = r // NX, r % NX
    other = (1 - s, r, c)
    pending = []

    def go(copy):
        copy.start()
        pending.append(copy.wait_send)

    def on_x(o):
        xt = (x + o) % NX
        return (s, y * NX + xt, c), xt

    def on_y(o):
        yt = (y + o) % NY
        return (s, yt * NX + x, c), yt

    def on_z(o):
        zt = (c + o) % NZ
        return (s, r, zt), zt

    lead = pltpu.make_async_copy(obs_hbm.at[:, 0:2, :], obs_lead, lsem.at[2])
    lead.start()
    load_prior = pltpu.make_async_copy(prior_hbm.at[pl.ds(r * PRI, PRI)], prior, lsem.at[1])
    load_prior.start()
    load_obs = pltpu.make_async_copy(obs_hbm, obs, lsem.at[0])
    load_obs.start()

    barrier = pltpu.get_barrier_semaphore()
    peers = [on_z(o)[0] for o in range(1, NZ)] + [on_x(o)[0] for o in range(1, NX)]
    peers += [on_y(o)[0] for o in range(1, NY)] + [other]
    for peer in peers:
        pl.semaphore_signal(barrier, inc=1, device_id=peer, device_id_type=MESH)

    alive = lax.broadcasted_iota(jnp.int32, (OBS, 128), 0) < live[0, 0]
    first = jnp.full((PRI, 128), s, jnp.int32) == 0
    base = pl.multiple_of(x * ROWS, 8)
    lead.wait()
    load_prior.wait()
    for h in range(2):

        @pl.when(c == h)
        def _():
            for l in range(2):
                lanes = slice(256 * h + 128 * l, 256 * h + 128 * l + 128)
                pan[pl.ds(base, OBS), lanes] = jnp.where(alive, obs_lead[:, l, :], 0.0)
                pan[pl.ds(base + OBS, PRI), lanes] = jnp.where(first, prior[:, l, :], 0.0)

    pl.semaphore_wait(barrier, len(peers))

    def piece(h, i, xs):
        start = pl.multiple_of(xs * ROWS + i * CH, 8)
        return pan.at[pl.ds(start, CH), 256 * h : 256 * h + 256]

    below = jnp.where(c == 0, NZ - 1, jnp.where(c <= NZ // 2, c + 1, c - 1))
    ends = (c == NZ // 2) | (c == NZ // 2 + 1)

    def down(h, i):
        return rcopy(piece(h, i, x), piece(h, i, x), zs.at[h, i], zr.at[h, i], (s, r, below))

    def cross(h, i):
        return rcopy(piece(h, i, x), piece(h, i, x), zs.at[h + 2, i], zr.at[h, i], (s, r, 1 - h))

    def settle(h, i):
        @pl.when(c == h)
        def _():
            cross(h, i).wait_send()

        @pl.when((c == h) | jnp.logical_not(ends))
        def _():
            down(h, i).wait_send()

    for i in range(CHUNKS):
        for h in range(2):

            @pl.when(c == h)
            def _():
                cross(h, i).start()
                down(h, i).start()

            pending.append(functools.partial(settle, h, i))

    load_obs.wait()

    def across(j, o):
        device, xt = on_x(o)
        return rcopy(
            xv.at[xt * 2 + j], xo.at[j, pl.ds(base, ROWS), :], xos.at[j, o - 1], xor_.at[j, x], device
        )

    def from_across(j, o):
        device, xs = on_x(o)
        rows = pl.ds(pl.multiple_of(xs * ROWS, 8), ROWS)
        return rcopy(xv.at[x * 2 + j], xo.at[j, rows, :], xos.at[j, o - 1], xor_.at[j, xs], device)

    for j in range(2):
        for xt in range(NX):
            cyc = xt * 2 + j
            for half in range(2):
                l = cyc * 2 + half
                lanes = slice(128 * half, 128 * half + 128)
                xv[cyc, 0:OBS, lanes] = jnp.where(alive, obs[:, l, :], 0.0)
                xv[cyc, OBS:ROWS, lanes] = jnp.where(first, prior[:, l, :], 0.0)
        if j == 0:
            for o in (1, 3, 2):
                go(across(j, o))
        xo[j, pl.ds(base, ROWS), :] = xv[x * 2 + j]

    for i in range(CHUNKS):
        for h in range(2):

            @pl.when(c != h)
            def _():
                down(h, i).wait_recv()

                @pl.when(jnp.logical_not(ends))
                def _():
                    down(h, i).start()

    xlane = pl.multiple_of(x * 128, 128)
    near = (c + 1) % NZ < 4
    crow = pl.multiple_of((c + 1) % 4 * 32, 8)

    def d0(o):
        device, xt = on_x(o)
        columns = pl.ds(pl.multiple_of(xt * 128, 128), 128)
        return rcopy(dfull.at[:, pl.ds(crow, 32), columns], xgot.at[x], d0s.at[o - 1], d0r.at[x], device)

    def from_d0(o):
        device, xf = on_x(o)
        return rcopy(dfull.at[:, pl.ds(crow, 32), pl.ds(xlane, 128)], xgot.at[xf], d0s.at[o - 1], d0r.at[xf], device)

    @pl.when(near)
    def _():
        for k in range(4):
            dfull[k] = dot(pan[pl.ds(base, ROWS), 128 * k : 128 * k + 128], pan[pl.ds(base, ROWS), :], 0, 0)
        for o in range(1, NX):
            d0(o).start()
        xgot[x] = dfull[:, pl.ds(crow, 32), pl.ds(xlane, 128)]

    def side(h, o):
        device, xt = on_x(o)
        rows = pan.at[pl.ds(base, ROWS), 256 * h : 256 * h + 256]
        return rcopy(rows, rows, xps.at[o - 1, h], xpr.at[x, h], device)

    def from_side(h, o):
        device, xs = on_x(o)
        rows = pan.at[pl.ds(pl.multiple_of(xs * ROWS, 8), ROWS), 256 * h : 256 * h + 256]
        return rcopy(rows, rows, xps.at[o - 1, h], xpr.at[xs, h], device)

    for o in (1, 3, 2):
        for h in range(2):
            go(side(h, o))
    for o in (1, 3, 2):
        go(across(1, o))

    def d1(k, o):
        device, yt = on_y(o)
        return rcopy(dpart.at[k], dgot.at[k, y], d1s.at[k, o - 1], d1r.at[k, y], device)

    def from_d1(k, o):
        device, yf = on_y(o)
        return rcopy(dpart.at[k], dgot.at[k, yf], d1s.at[k, o - 1], d1r.at[k, yf], device)

    def swap_d(k):
        return rcopy(dsum.at[k], dother.at[k], ss.at[k], sr.at[k], other)

    def dz(k, o):
        device, zt = on_z(o)
        place = info.at[k, pl.ds(crow, 32), pl.ds(xlane, 128)]
        return rcopy(dsum.at[k], place, dzs.at[k, o - 1], dzr.at[k, c], device)

    def from_dz(k, o):
        device, zf = on_z(o)
        place = info.at[k, pl.ds(pl.multiple_of((zf + 1) % 4 * 32, 8), 32), pl.ds(xlane, 128)]
        return rcopy(dsum.at[k], place, dzs.at[k, o - 1], dzr.at[k, zf], device), (zf + 1) % NZ < 4

    def dx(k, o):
        device, xt = on_x(o)
        place = info.at[k, :, pl.ds(xlane, 128)]
        return rcopy(place, place, dxs.at[k, o - 1], dxr.at[k, x], device)

    def from_dx(k, o):
        device, xf = on_x(o)
        place = info.at[k, :, pl.ds(pl.multiple_of(xf * 128, 128), 128)]
        return rcopy(place, place, dxs.at[k, o - 1], dxr.at[k, xf], device), xf >= k

    second = jnp.full((32, 128), s, jnp.int32) == 1

    @pl.when(near)
    def _():
        for o in range(1, NX):
            from_d0(o).wait_recv()
        dpart[...] = xgot[0] + xgot[1] + xgot[2] + xgot[3]
        for k in range(4):

            @pl.when(x >= k)
            def _():
                for o in range(1, NY):
                    d1(k, o).start()
                dgot[k, y] = dpart[k]

    def reduce_pivot(k):
        @pl.when(near & (x >= k))
        def _():
            for o in range(1, NY):
                from_d1(k, o).wait_recv()
            total = dgot[k, 0]
            for o in range(1, NY):
                total = total + dgot[k, o]
            dsum[k] = total
            swap_d(k).start()

    def spread_pivot(k):
        @pl.when(near & (x >= k))
        def _():
            swap_d(k).wait()
            dsum[k] = dsum[k] + jnp.where(second, dother[k], 0.0)
            for o in range(1, NZ):
                dz(k, o).start()
            info[k, pl.ds(crow, 32), pl.ds(xlane, 128)] = dsum[k]

    def share_pivot(k):
        @pl.when(x >= k)
        def _():
            for o in range(1, NZ):
                copy, sent = from_dz(k, o)
                pl.when(sent)(copy.wait_recv)
            for o in range(1, NX):
                dx(k, o).start()

    def take_pivot(k):
        for o in range(1, NX):
            copy, sent = from_dx(k, o)
            pl.when(sent)(copy.wait_recv)

    def settle_pivot():
        @pl.when(near)
        def _():
            for o in range(1, NX):
                d0(o).wait_send()

        for k in range(4):

            @pl.when(near & (x >= k))
            def _():
                for o in range(1, NY):
                    d1(k, o).wait_send()
                for o in range(1, NZ):
                    dz(k, o).wait_send()

            @pl.when(x >= k)
            def _():
                for o in range(1, NX):
                    dx(k, o).wait_send()

    pending.append(settle_pivot)

    def b1(j, o):
        device, yt = on_y(o)
        rows = bt.at[j, pl.ds(pl.multiple_of(yt * 32, 8), 32), :]
        return rcopy(rows, bgot.at[y, j], ys.at[j, o - 1], yr.at[j, y], device)

    def from_b1(j, o):
        device, yf = on_y(o)
        rows = bt.at[j, pl.ds(pl.multiple_of(yf * 32, 8), 32), :]
        return rcopy(rows, bgot.at[yf, j], ys.at[j, o - 1], yr.at[j, yf], device)

    def gram(j):
        for o in range(1, NX):
            from_across(j, o).wait_recv()
        for t in range(2):
            bt[j, 128 * t : 128 * t + 128, :] = dot(xo[j, :, 128 * t : 128 * t + 128], pan[...], 0, 0)
        for o in range(1, NY):
            go(b1(j, o))
        bgot[y, j] = bt[j, pl.ds(pl.multiple_of(y * 32, 8), 32), :]

    reduce_pivot(0)
    spread_pivot(0)
    for h in range(2):
        for o in range(1, NX):
            from_side(h, o).wait_recv()
    gram(0)
    share_pivot(0)
    for k in range(1, 4):
        reduce_pivot(k)
    for k in range(1, 4):
        spread_pivot(k)
    gram(1)
    for k in range(1, 4):
        share_pivot(k)

    def push(q):
        rows = solved.at[pl.ds(pl.multiple_of(q * 16, 8), 16), :]
        return rcopy(rows, got.at[r], rs.at[q], rr.at[r], (s, q, c))

    def pull(q):
        rows = solved.at[pl.ds(pl.multiple_of(q * 16, 8), 16), :]
        return rcopy(rows, got.at[q], rs.at[q], rr.at[q], (s, q, c))

    def solve(k):
        start = pl.multiple_of(k * 128, 128)
        solved[pl.ds(start, 128), :] = dot(linv[k], shares[:, pl.ds(start, 128)], 1, 1)

        def send(i, carry):
            q = k * 8 + i

            @pl.when(q != r)
            def _():
                push(q).start()

            @pl.when(q == r)
            def _():
                got[r] = solved[pl.ds(pl.multiple_of(r * 16, 8), 16), :]

            return carry

        lax.fori_loop(0, 8, send, 0)

    def eliminate(k):
        start = pl.multiple_of(k * 128, 128)
        shares[...] = shares[...] - dot(solved[pl.ds(start, 128), :], w[k], 0, 0)

    take_pivot(0)
    a[...] = jnp.zeros_like(a)
    a[0] = info[0]

    def panel(k, carry):
        start = pl.multiple_of(k * 128, 128)
        rows = [a[k, 8 * g : 8 * g + 8, pl.ds(start, 128)] for g in range(16)]
        right = inverse_factor(rows)
        for g in range(16):
            linv[k, 8 * g : 8 * g + 8, :] = right[g]

        @pl.when(k == 0)
        def _():
            for i in range(1, 4):
                take_pivot(i)
                a[i, :, 128 * i : 512] = info[i, :, 128 * i : 512]

        @pl.when(k < 3)
        def _():
            w[k] = dot(linv[k], a[k], 1, 0)
            for i in range(1, 4):
                right_of = slice(128 * i, 512)
                a[i, :, right_of] = a[i, :, right_of] - dot(
                    w[k, :, 128 * i : 128 * i + 128], w[k, :, right_of], 0, 0
                )

        @pl.when(k == 2)
        def _():
            for j in range(2):
                for o in range(1, NY):
                    from_b1(j, o).wait_recv()
                both = bgot[0, j]
                for o in range(1, NY):
                    both = both + bgot[o, j]
                shares[32 * j : 32 * j + 32, :] = both
            swap_b = rcopy(shares, bother, ss.at[4], sr.at[4], other)
            swap_b.start()
            swap_b.wait()
            later = jnp.full((64, 512), s, jnp.int32) == 1
            shares[...] = shares[...] + jnp.where(later, bother[...], 0.0)
            for j in range(3):
                solve(j)
                eliminate(j)

        return carry

    lax.fori_loop(0, 4, panel, 0)
    solve(3)

    for wait in pending:
        wait()

    def finish(o, carry):
        q = (r + o) % NR
        pull(q).wait_recv()
        push(q).wait_send()
        return carry

    lax.fori_loop(1, NR, finish, 0)


def assemble_kernel(got, out):
    r, c = lax.axis_index("row"), lax.axis_index("col")
    row_ids = r * 16 + lax.broadcasted_iota(jnp.int32, (16, 128), 0)
    lanes = lax.broadcasted_iota(jnp.int32, (16, 128), 1)
    for l in range(16):
        cyc, half = l // 2, l % 2
        xs, y0, lane0 = cyc // 2, half * 4, cyc % 2 * 32
        both = jnp.concatenate([got[(y0 + q) * NX + xs, :, lane0 : lane0 + 32] for q in range(4)], axis=1)
        column_ids = (cyc * NZ + c) * 256 + half * 128 + lanes
        out[:, l, :] = jnp.where(column_ids >= row_ids, both, 0.0)


def on_device(prior_root, observations, live_rows):
    vmem = pl.BlockSpec(memory_space=pltpu.VMEM)
    hbm = pl.BlockSpec(memory_space=pltpu.HBM)

    def buf(*shape):
        return pltpu.VMEM(shape, F32)

    def dma(*shape):
        return pltpu.SemaphoreType.DMA(shape)

    got = pl.pallas_call(
        update_kernel,
        out_shape=jax.ShapeDtypeStruct((NR, 16, 64), F32),
        in_specs=[pl.BlockSpec(memory_space=pltpu.SMEM), hbm, hbm],
        out_specs=vmem,
        scratch_shapes=[
            buf(OBS, 16, 128), buf(OBS, 2, 128), buf(PRI, 16, 128), buf(8, ROWS, 256), buf(2, NX * ROWS, 256),
            buf(NX * ROWS, 512), buf(4, 128, 512), buf(NX, 4, 32, 128), buf(4, 32, 128), buf(4, NY, 32, 128),
            buf(4, 32, 128), buf(4, 32, 128), buf(4, 128, 512),
            buf(2, 256, 512), buf(NY, 2, 32, 512), buf(64, 512), buf(64, 512),
            buf(4, 128, 512), buf(4, 128, 128), buf(4, 128, 512), buf(512, 64),
            dma(3), dma(4, CHUNKS), dma(2, CHUNKS), dma(2, NX - 1), dma(2, NX),
            dma(NX - 1, 2), dma(NX, 2), dma(NX - 1), dma(NX), dma(4, NY - 1), dma(4, NY), dma(5), dma(5),
            dma(4, NZ - 1), dma(4, NZ), dma(4, NX - 1), dma(4, NX), dma(2, NY - 1), dma(2, NY), dma(NR), dma(NR),
        ],
        compiler_params=pltpu.CompilerParams(
            collective_id=0, has_side_effects=True, vmem_limit_bytes=60 << 20
        ),
        name="update",
    )(live_rows, observations.reshape(OBS, 16, 128), prior_root.reshape(512, 16, 128))
    rows = pl.pallas_call(
        assemble_kernel,
        out_shape=jax.ShapeDtypeStruct((16, 16, 128), F32),
        in_specs=[vmem],
        out_specs=vmem,
        name="assemble",
    )(got)
    return rows.reshape(1, 16, 8, 1, 256)


def solution(mesh):
    placed = (
        P(None, None, "col", None),
        P("section", "row", None, "col", None),
        P("section", "row"),
    )
    return jax.shard_map(
        on_device,
        mesh=mesh,
        in_specs=placed,
        out_specs=P("section", "row", None, "col", None),
        check_vma=False,
    )
```

```python
import functools

import jax
import jax.numpy as jnp
from jax import lax
from jax.experimental import pallas as pl
from jax.experimental.pallas import tpu as pltpu
from jax.sharding import PartitionSpec as P

F32 = jnp.float32
NX, NY, NZ, NS = 4, 8, 8, 2
NR = NX * NY
OBS = 128
PRI = 16
ROWS = OBS + PRI
CHUNKS = 3
CH = ROWS // CHUNKS
MESH = pl.DeviceIdType.MESH


def dot(a, b, ca, cb):
    return lax.dot_general(
        a, b, (((ca,), (cb,)), ((), ())), precision=lax.Precision.HIGHEST, preferred_element_type=F32
    )


def rcopy(src, dst, send, recv, device):
    return pltpu.make_async_remote_copy(
        src_ref=src, dst_ref=dst, send_sem=send, recv_sem=recv, device_id=device, device_id_type=MESH
    )


def inverse_factor(rows):
    groups, n = len(rows), rows[0].shape[1]
    lane = lax.broadcasted_iota(jnp.int32, (8, n), 1)
    sub = lax.broadcasted_iota(jnp.int32, (8, n), 0)
    left = list(rows)
    right = [jnp.where(lane == sub + 8 * g, 1.0, 0.0).astype(F32) for g in range(groups)]
    for m in range(groups):
        cols = {
            g: [jnp.broadcast_to(left[g][:, 8 * m + j : 8 * m + j + 1], (8, n)) for j in range(8)]
            for g in range(m, groups)
        }
        pivot = {
            (i, j): jnp.broadcast_to(cols[m][j][i : i + 1, :], (8, n)) for j in range(8) for i in range(j, 8)
        }
        top_left = [jnp.broadcast_to(left[m][j : j + 1, :], (8, n)) for j in range(8)]
        top_right = [jnp.broadcast_to(right[m][j : j + 1, :], (8, n)) for j in range(8)]
        for j in range(8):
            scale = lax.rsqrt(pivot[j, j])
            top_left[j] = top_left[j] * scale
            top_right[j] = top_right[j] * scale
            for i in range(j + 1, 8):
                pivot[i, j] = pivot[i, j] * scale
            for g in range(m + 1, groups):
                cols[g][j] = cols[g][j] * scale
            for k in range(j + 1, 8):
                factor = pivot[k, j]
                for i in range(k, 8):
                    pivot[i, k] = pivot[i, k] - pivot[i, j] * factor
                top_left[k] = top_left[k] - top_left[j] * factor
                top_right[k] = top_right[k] - top_right[j] * factor
                for g in range(m + 1, groups):
                    cols[g][k] = cols[g][k] - cols[g][j] * factor
        for g in range(m + 1, groups):
            from_left, from_right = cols[g][0] * top_left[0], cols[g][0] * top_right[0]
            for j in range(1, 8):
                from_left = from_left + cols[g][j] * top_left[j]
                from_right = from_right + cols[g][j] * top_right[j]
            left[g] = left[g] - from_left
            right[g] = right[g] - from_right
        done = top_right[0]
        for j in range(1, 8):
            done = jnp.where(sub == j, top_right[j], done)
        right[m] = done
    return right


def update_kernel(
    live, obs_hbm, prior_hbm, got,
    obs, obs_lead, prior, xv, xo, pan, dfull, xgot, dpart, dgot, dsum, dother, info,
    bt, bgot, shares, bother, a, linv, w, solved,
    lsem, zs, zr, xos, xor_, xps, xpr, d0s, d0r, d1s, d1r, ss, sr, dzs, dzr, dxs, dxr, ys, yr, rs, rr,
):
    s, r, c = lax.axis_index("section"), lax.axis_index("row"), lax.axis_index("col")
    y, x = r // NX, r % NX
    other = (1 - s, r, c)
    pending = []

    def go(copy):
        copy.start()
        pending.append(copy.wait_send)

    def on_x(o):
        xt = (x + o) % NX
        return (s, y * NX + xt, c), xt

    def on_y(o):
        yt = (y + o) % NY
        return (s, yt * NX + x, c), yt

    def on_z(o):
        zt = (c + o) % NZ
        return (s, r, zt), zt

    lead = pltpu.make_async_copy(obs_hbm.at[:, 0:2, :], obs_lead, lsem.at[2])
    lead.start()
    load_prior = pltpu.make_async_copy(prior_hbm.at[pl.ds(r * PRI, PRI)], prior, lsem.at[1])
    load_prior.start()
    load_obs = pltpu.make_async_copy(obs_hbm, obs, lsem.at[0])
    load_obs.start()

    barrier = pltpu.get_barrier_semaphore()
    peers = [on_z(o)[0] for o in range(1, NZ)] + [on_x(o)[0] for o in range(1, NX)]
    peers += [on_y(o)[0] for o in range(1, NY)] + [other]
    for peer in peers:
        pl.semaphore_signal(barrier, inc=1, device_id=peer, device_id_type=MESH)

    alive = lax.broadcasted_iota(jnp.int32, (OBS, 128), 0) < live[0, 0]
    first = jnp.full((PRI, 128), s, jnp.int32) == 0
    base = pl.multiple_of(x * ROWS, 8)
    lead.wait()
    load_prior.wait()
    for h in range(2):

        @pl.when(c == h)
        def _():
            for l in range(2):
                lanes = slice(256 * h + 128 * l, 256 * h + 128 * l + 128)
                pan[pl.ds(base, OBS), lanes] = jnp.where(alive, obs_lead[:, l, :], 0.0)
                pan[pl.ds(base + OBS, PRI), lanes] = jnp.where(first, prior[:, l, :], 0.0)

    pl.semaphore_wait(barrier, len(peers))

    def piece(h, i, xs):
        start = pl.multiple_of(xs * ROWS + i * CH, 8)
        return pan.at[pl.ds(start, CH), 256 * h : 256 * h + 256]

    below = jnp.where(c == 0, NZ - 1, jnp.where(c <= NZ // 2, c + 1, c - 1))
    ends = (c == NZ // 2) | (c == NZ // 2 + 1)

    def down(h, i):
        return rcopy(piece(h, i, x), piece(h, i, x), zs.at[h, i], zr.at[h, i], (s, r, below))

    def cross(h, i):
        return rcopy(piece(h, i, x), piece(h, i, x), zs.at[h + 2, i], zr.at[h, i], (s, r, 1 - h))

    def settle(h, i):
        @pl.when(c == h)
        def _():
            cross(h, i).wait_send()

        @pl.when((c == h) | jnp.logical_not(ends))
        def _():
            down(h, i).wait_send()

    for i in range(CHUNKS):
        for h in range(2):

            @pl.when(c == h)
            def _():
                cross(h, i).start()
                down(h, i).start()

            pending.append(functools.partial(settle, h, i))

    load_obs.wait()

    def across(j, o):
        device, xt = on_x(o)
        return rcopy(
            xv.at[xt * 2 + j], xo.at[j, pl.ds(base, ROWS), :], xos.at[j, o - 1], xor_.at[j, x], device
        )

    def from_across(j, o):
        device, xs = on_x(o)
        rows = pl.ds(pl.multiple_of(xs * ROWS, 8), ROWS)
        return rcopy(xv.at[x * 2 + j], xo.at[j, rows, :], xos.at[j, o - 1], xor_.at[j, xs], device)

    for j in range(2):
        for xt in range(NX):
            cyc = xt * 2 + j
            for half in range(2):
                l = cyc * 2 + half
                lanes = slice(128 * half, 128 * half + 128)
                xv[cyc, 0:OBS, lanes] = jnp.where(alive, obs[:, l, :], 0.0)
                xv[cyc, OBS:ROWS, lanes] = jnp.where(first, prior[:, l, :], 0.0)
        if j == 0:
            for o in (1, 3, 2):
                go(across(j, o))
        xo[j, pl.ds(base, ROWS), :] = xv[x * 2 + j]

    for i in range(CHUNKS):
        for h in range(2):

            @pl.when(c != h)
            def _():
                down(h, i).wait_recv()

                @pl.when(jnp.logical_not(ends))
                def _():
                    down(h, i).start()

    xlane = pl.multiple_of(x * 128, 128)
    near = (c + 1) % NZ < 4
    crow = pl.multiple_of((c + 1) % 4 * 32, 8)

    def block(xt, t):
        if t == 0:
            return 0, xt
        if t == 1:
            return jnp.where(xt < 3, 1, 2), jnp.where(xt < 3, xt + 1, 2)
        return 2 + xt % 2, 3

    def has(xt, t):
        return xt < (2 if t == 2 else NX)

    def lanes_of(l):
        return pl.ds(pl.multiple_of(l * 128, 128), 128)

    def d0(t, o):
        device, xt = on_x(o)
        k, l = block(xt, t)
        part = dfull.at[k, pl.ds(crow, 32), lanes_of(l)]
        return rcopy(part, xgot.at[t, x], d0s.at[t, o - 1], d0r.at[t, x], device), has(xt, t)

    def from_d0(t, o):
        device, xf = on_x(o)
        k, l = block(x, t)
        part = dfull.at[k, pl.ds(crow, 32), lanes_of(l)]
        return rcopy(part, xgot.at[t, xf], d0s.at[t, o - 1], d0r.at[t, xf], device)

    @pl.when(near)
    def _():
        for k in range(4):
            cut = slice(128 * k, 512)
            dfull[k, :, cut] = dot(pan[pl.ds(base, ROWS), 128 * k : 128 * k + 128], pan[pl.ds(base, ROWS), cut], 0, 0)
            if k == 0:
                for o in range(1, NX):
                    d0(0, o)[0].start()
        for t in (1, 2):
            for o in range(1, NX):
                copy, wanted = d0(t, o)
                pl.when(wanted)(copy.start)
        for t in range(3):
            k, l = block(x, t)
            xgot[t, x] = dfull[k, pl.ds(crow, 32), lanes_of(l)]

    def side(h, o):
        device, xt = on_x(o)
        rows = pan.at[pl.ds(base, ROWS), 256 * h : 256 * h + 256]
        return rcopy(rows, rows, xps.at[o - 1, h], xpr.at[x, h], device)

    def from_side(h, o):
        device, xs = on_x(o)
        rows = pan.at[pl.ds(pl.multiple_of(xs * ROWS, 8), ROWS), 256 * h : 256 * h + 256]
        return rcopy(rows, rows, xps.at[o - 1, h], xpr.at[xs, h], device)

    for o in (1, 3, 2):
        for h in range(2):
            go(side(h, o))
    for o in (1, 3, 2):
        go(across(1, o))

    def d1(t, o):
        device, yt = on_y(o)
        return rcopy(dpart.at[t], dgot.at[t, y], d1s.at[t, o - 1], d1r.at[t, y], device)

    def from_d1(t, o):
        device, yf = on_y(o)
        return rcopy(dpart.at[t], dgot.at[t, yf], d1s.at[t, o - 1], d1r.at[t, yf], device)

    def swap_d(t):
        return rcopy(dsum.at[t], dother.at[t], ss.at[t], sr.at[t], other)

    def dz(t, o):
        device, zt = on_z(o)
        k, l = block(x, t)
        place = info.at[k, pl.ds(crow, 32), lanes_of(l)]
        return rcopy(dsum.at[t], place, dzs.at[t, o - 1], dzr.at[t, c], device)

    def from_dz(t, o):
        device, zf = on_z(o)
        k, l = block(x, t)
        place = info.at[k, pl.ds(pl.multiple_of((zf + 1) % 4 * 32, 8), 32), lanes_of(l)]
        return rcopy(dsum.at[t], place, dzs.at[t, o - 1], dzr.at[t, zf], device), (zf + 1) % NZ < 4

    def dx(t, o):
        device, xt = on_x(o)
        k, l = block(x, t)
        place = info.at[k, :, lanes_of(l)]
        return rcopy(place, place, dxs.at[t, o - 1], dxr.at[t, x], device)

    def from_dx(t, o):
        device, xf = on_x(o)
        k, l = block(xf, t)
        place = info.at[k, :, lanes_of(l)]
        return rcopy(place, place, dxs.at[t, o - 1], dxr.at[t, xf], device), has(xf, t)

    second = jnp.full((32, 128), s, jnp.int32) == 1

    def begin_pivot(t):
        @pl.when(near & has(x, t))
        def _():
            for o in range(1, NX):
                from_d0(t, o).wait_recv()
            dpart[t] = xgot[t, 0] + xgot[t, 1] + xgot[t, 2] + xgot[t, 3]
            for o in range(1, NY):
                d1(t, o).start()
            dgot[t, y] = dpart[t]

    for t in range(3):
        begin_pivot(t)

    def reduce_pivot(t):
        @pl.when(near & has(x, t))
        def _():
            for o in range(1, NY):
                from_d1(t, o).wait_recv()
            total = dgot[t, 0]
            for o in range(1, NY):
                total = total + dgot[t, o]
            dsum[t] = total
            swap_d(t).start()

    def spread_pivot(t):
        @pl.when(near & has(x, t))
        def _():
            swap_d(t).wait()
            dsum[t] = dsum[t] + jnp.where(second, dother[t], 0.0)
            for o in range(1, NZ):
                dz(t, o).start()
            k, l = block(x, t)
            info[k, pl.ds(crow, 32), lanes_of(l)] = dsum[t]

    def share_pivot(t):
        @pl.when(has(x, t))
        def _():
            for o in range(1, NZ):
                copy, sent = from_dz(t, o)
                pl.when(sent)(copy.wait_recv)
            for o in range(1, NX):
                dx(t, o).start()

    def take_pivot(t):
        for o in range(1, NX):
            copy, sent = from_dx(t, o)
            pl.when(sent)(copy.wait_recv)

    def settle_pivot():
        for t in range(3):

            @pl.when(near)
            def _():
                for o in range(1, NX):
                    copy, wanted = d0(t, o)
                    pl.when(wanted)(copy.wait_send)

            @pl.when(near & has(x, t))
            def _():
                for o in range(1, NY):
                    d1(t, o).wait_send()
                for o in range(1, NZ):
                    dz(t, o).wait_send()

            @pl.when(has(x, t))
            def _():
                for o in range(1, NX):
                    dx(t, o).wait_send()

    pending.append(settle_pivot)

    def b1(j, o):
        device, yt = on_y(o)
        rows = bt.at[j, pl.ds(pl.multiple_of(yt * 32, 8), 32), :]
        return rcopy(rows, bgot.at[y, j], ys.at[j, o - 1], yr.at[j, y], device)

    def from_b1(j, o):
        device, yf = on_y(o)
        rows = bt.at[j, pl.ds(pl.multiple_of(yf * 32, 8), 32), :]
        return rcopy(rows, bgot.at[yf, j], ys.at[j, o - 1], yr.at[j, yf], device)

    def gram(j):
        for o in range(1, NX):
            from_across(j, o).wait_recv()
        for t in range(2):
            bt[j, 128 * t : 128 * t + 128, :] = dot(xo[j, :, 128 * t : 128 * t + 128], pan[...], 0, 0)
        for o in range(1, NY):
            go(b1(j, o))
        bgot[y, j] = bt[j, pl.ds(pl.multiple_of(y * 32, 8), 32), :]

    reduce_pivot(0)
    spread_pivot(0)
    for h in range(2):
        for o in range(1, NX):
            from_side(h, o).wait_recv()
    gram(0)
    share_pivot(0)
    for t in (1, 2):
        reduce_pivot(t)
    for t in (1, 2):
        spread_pivot(t)
    gram(1)

    def push(q):
        rows = solved.at[pl.ds(pl.multiple_of(q * 16, 8), 16), :]
        return rcopy(rows, got.at[r], rs.at[q], rr.at[r], (s, q, c))

    def pull(q):
        rows = solved.at[pl.ds(pl.multiple_of(q * 16, 8), 16), :]
        return rcopy(rows, got.at[q], rs.at[q], rr.at[q], (s, q, c))

    def solve(k):
        start = pl.multiple_of(k * 128, 128)
        solved[pl.ds(start, 128), :] = dot(linv[k], shares[:, pl.ds(start, 128)], 1, 1)

        def send(i, carry):
            q = k * 8 + i

            @pl.when(q != r)
            def _():
                push(q).start()

            @pl.when(q == r)
            def _():
                got[r] = solved[pl.ds(pl.multiple_of(r * 16, 8), 16), :]

            return carry

        lax.fori_loop(0, 8, send, 0)

    def eliminate(k):
        start = pl.multiple_of(k * 128, 128)
        shares[...] = shares[...] - dot(solved[pl.ds(start, 128), :], w[k], 0, 0)

    def swap_b():
        return rcopy(shares, bother, ss.at[4], sr.at[4], other)

    a[...] = jnp.zeros_like(a)
    take_pivot(0)
    a[0] = info[0]

    def panel(k, carry):
        start = pl.multiple_of(k * 128, 128)
        rows = [a[k, 8 * g : 8 * g + 8, pl.ds(start, 128)] for g in range(16)]
        right = inverse_factor(rows)
        for g in range(16):
            linv[k, 8 * g : 8 * g + 8, :] = right[g]

        @pl.when(k == 0)
        def _():
            for t in (1, 2):
                share_pivot(t)
            for t in (1, 2):
                take_pivot(t)
            for i in range(1, 4):
                a[i, :, 128 * i : 512] = info[i, :, 128 * i : 512]

        @pl.when(k < 3)
        def _():
            w[k] = dot(linv[k], a[k], 1, 0)
            for i in range(1, 4):
                right_of = slice(128 * i, 512)
                a[i, :, right_of] = a[i, :, right_of] - dot(
                    w[k, :, 128 * i : 128 * i + 128], w[k, :, right_of], 0, 0
                )

        @pl.when(k == 1)
        def _():
            for j in range(2):
                for o in range(1, NY):
                    from_b1(j, o).wait_recv()
                both = bgot[0, j]
                for o in range(1, NY):
                    both = both + bgot[o, j]
                shares[32 * j : 32 * j + 32, :] = both
            swap_b().start()

        @pl.when(k == 2)
        def _():
            swap_b().wait()
            later = jnp.full((64, 512), s, jnp.int32) == 1
            shares[...] = shares[...] + jnp.where(later, bother[...], 0.0)
            for j in range(3):
                solve(j)
                eliminate(j)

        return carry

    lax.fori_loop(0, 4, panel, 0)
    solve(3)

    for wait in pending:
        wait()

    def finish(o, carry):
        q = (r + o) % NR
        pull(q).wait_recv()
        push(q).wait_send()
        return carry

    lax.fori_loop(1, NR, finish, 0)


def assemble_kernel(got, out):
    r, c = lax.axis_index("row"), lax.axis_index("col")
    row_ids = r * 16 + lax.broadcasted_iota(jnp.int32, (16, 128), 0)
    lanes = lax.broadcasted_iota(jnp.int32, (16, 128), 1)
    for l in range(16):
        cyc, half = l // 2, l % 2
        xs, y0, lane0 = cyc // 2, half * 4, cyc % 2 * 32
        both = jnp.concatenate([got[(y0 + q) * NX + xs, :, lane0 : lane0 + 32] for q in range(4)], axis=1)
        column_ids = (cyc * NZ + c) * 256 + half * 128 + lanes
        out[:, l, :] = jnp.where(column_ids >= row_ids, both, 0.0)


def on_device(prior_root, observations, live_rows):
    vmem = pl.BlockSpec(memory_space=pltpu.VMEM)
    hbm = pl.BlockSpec(memory_space=pltpu.HBM)

    def buf(*shape):
        return pltpu.VMEM(shape, F32)

    def dma(*shape):
        return pltpu.SemaphoreType.DMA(shape)

    got = pl.pallas_call(
        update_kernel,
        out_shape=jax.ShapeDtypeStruct((NR, 16, 64), F32),
        in_specs=[pl.BlockSpec(memory_space=pltpu.SMEM), hbm, hbm],
        out_specs=vmem,
        scratch_shapes=[
            buf(OBS, 16, 128), buf(OBS, 2, 128), buf(PRI, 16, 128), buf(8, ROWS, 256), buf(2, NX * ROWS, 256),
            buf(NX * ROWS, 512), buf(4, 128, 512), buf(3, NX, 32, 128), buf(3, 32, 128), buf(3, NY, 32, 128),
            buf(3, 32, 128), buf(3, 32, 128), buf(4, 128, 512),
            buf(2, 256, 512), buf(NY, 2, 32, 512), buf(64, 512), buf(64, 512),
            buf(4, 128, 512), buf(4, 128, 128), buf(4, 128, 512), buf(512, 64),
            dma(3), dma(4, CHUNKS), dma(2, CHUNKS), dma(2, NX - 1), dma(2, NX),
            dma(NX - 1, 2), dma(NX, 2), dma(3, NX - 1), dma(3, NX), dma(3, NY - 1), dma(3, NY), dma(5), dma(5),
            dma(3, NZ - 1), dma(3, NZ), dma(3, NX - 1), dma(3, NX), dma(2, NY - 1), dma(2, NY), dma(NR), dma(NR),
        ],
        compiler_params=pltpu.CompilerParams(
            collective_id=0, has_side_effects=True, vmem_limit_bytes=60 << 20
        ),
        name="update",
    )(live_rows, observations.reshape(OBS, 16, 128), prior_root.reshape(512, 16, 128))
    rows = pl.pallas_call(
        assemble_kernel,
        out_shape=jax.ShapeDtypeStruct((16, 16, 128), F32),
        in_specs=[vmem],
        out_specs=vmem,
        name="assemble",
    )(got)
    return rows.reshape(1, 16, 8, 1, 256)


def solution(mesh):
    placed = (
        P(None, None, "col", None),
        P("section", "row", None, "col", None),
        P("section", "row"),
    )
    return jax.shard_map(
        on_device,
        mesh=mesh,
        in_specs=placed,
        out_specs=P("section", "row", None, "col", None),
        check_vma=False,
    )
```

```python
import functools

import jax
import jax.numpy as jnp
from jax import lax
from jax.experimental import pallas as pl
from jax.experimental.pallas import tpu as pltpu
from jax.sharding import PartitionSpec as P

F32 = jnp.float32
NX, NY, NZ, NS = 4, 8, 8, 2
NR = NX * NY
OBS = 128
PRI = 16
ROWS = OBS + PRI
CHUNKS = 6
CH = ROWS // CHUNKS
MESH = pl.DeviceIdType.MESH


def dot(a, b, ca, cb):
    return lax.dot_general(
        a, b, (((ca,), (cb,)), ((), ())), precision=lax.Precision.HIGHEST, preferred_element_type=F32
    )


def rcopy(src, dst, send, recv, device):
    return pltpu.make_async_remote_copy(
        src_ref=src, dst_ref=dst, send_sem=send, recv_sem=recv, device_id=device, device_id_type=MESH
    )


def inverse_factor(rows):
    groups, n = len(rows), rows[0].shape[1]
    lane = lax.broadcasted_iota(jnp.int32, (8, n), 1)
    sub = lax.broadcasted_iota(jnp.int32, (8, n), 0)
    left = list(rows)
    right = [jnp.where(lane == sub + 8 * g, 1.0, 0.0).astype(F32) for g in range(groups)]
    for m in range(groups):
        cols = {
            g: [jnp.broadcast_to(left[g][:, 8 * m + j : 8 * m + j + 1], (8, n)) for j in range(8)]
            for g in range(m, groups)
        }
        pivot = {
            (i, j): jnp.broadcast_to(cols[m][j][i : i + 1, :], (8, n)) for j in range(8) for i in range(j, 8)
        }
        top_left = [jnp.broadcast_to(left[m][j : j + 1, :], (8, n)) for j in range(8)]
        top_right = [jnp.broadcast_to(right[m][j : j + 1, :], (8, n)) for j in range(8)]
        for j in range(8):
            scale = lax.rsqrt(pivot[j, j])
            top_left[j] = top_left[j] * scale
            top_right[j] = top_right[j] * scale
            for i in range(j + 1, 8):
                pivot[i, j] = pivot[i, j] * scale
            for g in range(m + 1, groups):
                cols[g][j] = cols[g][j] * scale
            for k in range(j + 1, 8):
                factor = pivot[k, j]
                for i in range(k, 8):
                    pivot[i, k] = pivot[i, k] - pivot[i, j] * factor
                top_left[k] = top_left[k] - top_left[j] * factor
                top_right[k] = top_right[k] - top_right[j] * factor
                for g in range(m + 1, groups):
                    cols[g][k] = cols[g][k] - cols[g][j] * factor
        for g in range(m + 1, groups):
            from_left, from_right = cols[g][0] * top_left[0], cols[g][0] * top_right[0]
            for j in range(1, 8):
                from_left = from_left + cols[g][j] * top_left[j]
                from_right = from_right + cols[g][j] * top_right[j]
            left[g] = left[g] - from_left
            right[g] = right[g] - from_right
        done = top_right[0]
        for j in range(1, 8):
            done = jnp.where(sub == j, top_right[j], done)
        right[m] = done
    return right


def update_kernel(
    live, obs_hbm, prior_hbm, got,
    obs, obs_lead, prior, xv, xo, pan, dfull, xgot, dpart, dgot, dsum, dother, info,
    bt, bgot, shares, bother, a, linv, w, solved,
    lsem, zs, zr, xos, xor_, xps, xpr, d0s, d0r, d1s, d1r, ss, sr, dzs, dzr, dxs, dxr, ys, yr, rs, rr,
):
    s, r, c = lax.axis_index("section"), lax.axis_index("row"), lax.axis_index("col")
    y, x = r // NX, r % NX
    other = (1 - s, r, c)
    pending = []

    def go(copy):
        copy.start()
        pending.append(copy.wait_send)

    def on_x(o):
        xt = (x + o) % NX
        return (s, y * NX + xt, c), xt

    def on_y(o):
        yt = (y + o) % NY
        return (s, yt * NX + x, c), yt

    def on_z(o):
        zt = (c + o) % NZ
        return (s, r, zt), zt

    lead = pltpu.make_async_copy(obs_hbm.at[:, 0:2, :], obs_lead, lsem.at[2])
    lead.start()
    load_prior = pltpu.make_async_copy(prior_hbm.at[pl.ds(r * PRI, PRI)], prior, lsem.at[1])
    load_prior.start()
    load_obs = pltpu.make_async_copy(obs_hbm, obs, lsem.at[0])
    load_obs.start()

    barrier = pltpu.get_barrier_semaphore()
    peers = [on_z(o)[0] for o in range(1, NZ)] + [on_x(o)[0] for o in range(1, NX)]
    peers += [on_y(o)[0] for o in range(1, NY)] + [other]
    for peer in peers:
        pl.semaphore_signal(barrier, inc=1, device_id=peer, device_id_type=MESH)

    alive = lax.broadcasted_iota(jnp.int32, (OBS, 128), 0) < live[0, 0]
    first = jnp.full((PRI, 128), s, jnp.int32) == 0
    base = pl.multiple_of(x * ROWS, 8)
    lead.wait()
    load_prior.wait()
    for h in range(2):

        @pl.when(c == h)
        def _():
            for l in range(2):
                lanes = slice(256 * h + 128 * l, 256 * h + 128 * l + 128)
                pan[pl.ds(base, OBS), lanes] = jnp.where(alive, obs_lead[:, l, :], 0.0)
                pan[pl.ds(base + OBS, PRI), lanes] = jnp.where(first, prior[:, l, :], 0.0)

    pl.semaphore_wait(barrier, len(peers))

    def piece(h, i, xs):
        start = pl.multiple_of(xs * ROWS + i * CH, 8)
        return pan.at[pl.ds(start, CH), 256 * h : 256 * h + 256]

    below = jnp.where(c == 0, NZ - 1, jnp.where(c <= NZ // 2, c + 1, c - 1))
    ends = (c == NZ // 2) | (c == NZ // 2 + 1)

    def down(h, i):
        return rcopy(piece(h, i, x), piece(h, i, x), zs.at[h, i], zr.at[h, i], (s, r, below))

    def cross(h, i):
        return rcopy(piece(h, i, x), piece(h, i, x), zs.at[h + 2, i], zr.at[h, i], (s, r, 1 - h))

    def settle(h, i):
        @pl.when(c == h)
        def _():
            cross(h, i).wait_send()

        @pl.when((c == h) | jnp.logical_not(ends))
        def _():
            down(h, i).wait_send()

    for i in range(CHUNKS):
        for h in range(2):

            @pl.when(c == h)
            def _():
                cross(h, i).start()
                down(h, i).start()

            pending.append(functools.partial(settle, h, i))

    load_obs.wait()

    def across(j, o):
        device, xt = on_x(o)
        return rcopy(
            xv.at[xt * 2 + j], xo.at[j, pl.ds(base, ROWS), :], xos.at[j, o - 1], xor_.at[j, x], device
        )

    def from_across(j, o):
        device, xs = on_x(o)
        rows = pl.ds(pl.multiple_of(xs * ROWS, 8), ROWS)
        return rcopy(xv.at[x * 2 + j], xo.at[j, rows, :], xos.at[j, o - 1], xor_.at[j, xs], device)

    for j in range(2):
        for xt in range(NX):
            cyc = xt * 2 + j
            for half in range(2):
                l = cyc * 2 + half
                lanes = slice(128 * half, 128 * half + 128)
                xv[cyc, 0:OBS, lanes] = jnp.where(alive, obs[:, l, :], 0.0)
                xv[cyc, OBS:ROWS, lanes] = jnp.where(first, prior[:, l, :], 0.0)
        if j == 0:
            for o in (1, 3, 2):
                go(across(j, o))
        xo[j, pl.ds(base, ROWS), :] = xv[x * 2 + j]

    for i in range(CHUNKS):
        for h in range(2):

            @pl.when(c != h)
            def _():
                down(h, i).wait_recv()

                @pl.when(jnp.logical_not(ends))
                def _():
                    down(h, i).start()

    xlane = pl.multiple_of(x * 128, 128)
    near = (c + 1) % NZ < 4
    crow = pl.multiple_of((c + 1) % 4 * 32, 8)

    def block(xt, t):
        if t == 0:
            return 0, xt
        if t == 1:
            return jnp.where(xt < 3, 1, 2), jnp.where(xt < 3, xt + 1, 2)
        return 2 + xt % 2, 3

    def has(xt, t):
        return xt < (2 if t == 2 else NX)

    def lanes_of(l):
        return pl.ds(pl.multiple_of(l * 128, 128), 128)

    def d0(t, o):
        device, xt = on_x(o)
        k, l = block(xt, t)
        part = dfull.at[k, pl.ds(crow, 32), lanes_of(l)]
        return rcopy(part, xgot.at[t, x], d0s.at[t, o - 1], d0r.at[t, x], device), has(xt, t)

    def from_d0(t, o):
        device, xf = on_x(o)
        k, l = block(x, t)
        part = dfull.at[k, pl.ds(crow, 32), lanes_of(l)]
        return rcopy(part, xgot.at[t, xf], d0s.at[t, o - 1], d0r.at[t, xf], device)

    @pl.when(near)
    def _():
        for k in range(4):
            cut = slice(128 * k, 512)
            dfull[k, :, cut] = dot(pan[pl.ds(base, ROWS), 128 * k : 128 * k + 128], pan[pl.ds(base, ROWS), cut], 0, 0)
            if k == 0:
                for o in range(1, NX):
                    d0(0, o)[0].start()
        for t in (1, 2):
            for o in range(1, NX):
                copy, wanted = d0(t, o)
                pl.when(wanted)(copy.start)
        for t in range(3):
            k, l = block(x, t)
            xgot[t, x] = dfull[k, pl.ds(crow, 32), lanes_of(l)]

    def side(h, o):
        device, xt = on_x(o)
        rows = pan.at[pl.ds(base, ROWS), 256 * h : 256 * h + 256]
        return rcopy(rows, rows, xps.at[o - 1, h], xpr.at[x, h], device)

    def from_side(h, o):
        device, xs = on_x(o)
        rows = pan.at[pl.ds(pl.multiple_of(xs * ROWS, 8), ROWS), 256 * h : 256 * h + 256]
        return rcopy(rows, rows, xps.at[o - 1, h], xpr.at[xs, h], device)

    for o in (1, 3, 2):
        for h in range(2):
            go(side(h, o))
    for o in (1, 3, 2):
        go(across(1, o))

    def d1(t, o):
        device, yt = on_y(o)
        return rcopy(dpart.at[t], dgot.at[t, y], d1s.at[t, o - 1], d1r.at[t, y], device)

    def from_d1(t, o):
        device, yf = on_y(o)
        return rcopy(dpart.at[t], dgot.at[t, yf], d1s.at[t, o - 1], d1r.at[t, yf], device)

    def swap_d(t):
        return rcopy(dsum.at[t], dother.at[t], ss.at[t], sr.at[t], other)

    def dz(t, o):
        device, zt = on_z(o)
        k, l = block(x, t)
        place = info.at[k, pl.ds(crow, 32), lanes_of(l)]
        return rcopy(dsum.at[t], place, dzs.at[t, o - 1], dzr.at[t, c], device)

    def from_dz(t, o):
        device, zf = on_z(o)
        k, l = block(x, t)
        place = info.at[k, pl.ds(pl.multiple_of((zf + 1) % 4 * 32, 8), 32), lanes_of(l)]
        return rcopy(dsum.at[t], place, dzs.at[t, o - 1], dzr.at[t, zf], device), (zf + 1) % NZ < 4

    def dx(t, o):
        device, xt = on_x(o)
        k, l = block(x, t)
        place = info.at[k, :, lanes_of(l)]
        return rcopy(place, place, dxs.at[t, o - 1], dxr.at[t, x], device)

    def from_dx(t, o):
        device, xf = on_x(o)
        k, l = block(xf, t)
        place = info.at[k, :, lanes_of(l)]
        return rcopy(place, place, dxs.at[t, o - 1], dxr.at[t, xf], device), has(xf, t)

    second = jnp.full((32, 128), s, jnp.int32) == 1

    def begin_pivot(t):
        @pl.when(near & has(x, t))
        def _():
            for o in range(1, NX):
                from_d0(t, o).wait_recv()
            dpart[t] = xgot[t, 0] + xgot[t, 1] + xgot[t, 2] + xgot[t, 3]
            for o in range(1, NY):
                d1(t, o).start()
            dgot[t, y] = dpart[t]

    for t in range(3):
        begin_pivot(t)

    def reduce_pivot(t):
        @pl.when(near & has(x, t))
        def _():
            for o in range(1, NY):
                from_d1(t, o).wait_recv()
            total = dgot[t, 0]
            for o in range(1, NY):
                total = total + dgot[t, o]
            dsum[t] = total
            swap_d(t).start()

    def spread_pivot(t):
        @pl.when(near & has(x, t))
        def _():
            swap_d(t).wait()
            dsum[t] = dsum[t] + jnp.where(second, dother[t], 0.0)
            for o in range(1, NZ):
                dz(t, o).start()
            k, l = block(x, t)
            info[k, pl.ds(crow, 32), lanes_of(l)] = dsum[t]

    def share_pivot(t):
        @pl.when(has(x, t))
        def _():
            for o in range(1, NZ):
                copy, sent = from_dz(t, o)
                pl.when(sent)(copy.wait_recv)
            for o in range(1, NX):
                dx(t, o).start()

    def take_pivot(t):
        for o in range(1, NX):
            copy, sent = from_dx(t, o)
            pl.when(sent)(copy.wait_recv)

    def settle_pivot():
        for t in range(3):

            @pl.when(near)
            def _():
                for o in range(1, NX):
                    copy, wanted = d0(t, o)
                    pl.when(wanted)(copy.wait_send)

            @pl.when(near & has(x, t))
            def _():
                for o in range(1, NY):
                    d1(t, o).wait_send()
                for o in range(1, NZ):
                    dz(t, o).wait_send()

            @pl.when(has(x, t))
            def _():
                for o in range(1, NX):
                    dx(t, o).wait_send()

    pending.append(settle_pivot)

    def b1(j, o):
        device, yt = on_y(o)
        rows = bt.at[j, pl.ds(pl.multiple_of(yt * 32, 8), 32), :]
        return rcopy(rows, bgot.at[y, j], ys.at[j, o - 1], yr.at[j, y], device)

    def from_b1(j, o):
        device, yf = on_y(o)
        rows = bt.at[j, pl.ds(pl.multiple_of(yf * 32, 8), 32), :]
        return rcopy(rows, bgot.at[yf, j], ys.at[j, o - 1], yr.at[j, yf], device)

    def gram(j):
        for o in range(1, NX):
            from_across(j, o).wait_recv()
        for t in range(2):
            bt[j, 128 * t : 128 * t + 128, :] = dot(xo[j, :, 128 * t : 128 * t + 128], pan[...], 0, 0)
        for o in range(1, NY):
            go(b1(j, o))
        bgot[y, j] = bt[j, pl.ds(pl.multiple_of(y * 32, 8), 32), :]

    reduce_pivot(0)
    spread_pivot(0)
    for h in range(2):
        for o in range(1, NX):
            from_side(h, o).wait_recv()
    gram(0)
    share_pivot(0)
    for t in (1, 2):
        reduce_pivot(t)
    for t in (1, 2):
        spread_pivot(t)
    gram(1)

    def push(q):
        rows = solved.at[pl.ds(pl.multiple_of(q * 16, 8), 16), :]
        return rcopy(rows, got.at[r], rs.at[q], rr.at[r], (s, q, c))

    def pull(q):
        rows = solved.at[pl.ds(pl.multiple_of(q * 16, 8), 16), :]
        return rcopy(rows, got.at[q], rs.at[q], rr.at[q], (s, q, c))

    def solve(k):
        start = pl.multiple_of(k * 128, 128)
        solved[pl.ds(start, 128), :] = dot(linv[k], shares[:, pl.ds(start, 128)], 1, 1)

        def send(i, carry):
            q = k * 8 + i

            @pl.when(q != r)
            def _():
                push(q).start()

            @pl.when(q == r)
            def _():
                got[r] = solved[pl.ds(pl.multiple_of(r * 16, 8), 16), :]

            return carry

        lax.fori_loop(0, 8, send, 0)

    def eliminate(k):
        start = pl.multiple_of(k * 128, 128)
        shares[...] = shares[...] - dot(solved[pl.ds(start, 128), :], w[k], 0, 0)

    def swap_b():
        return rcopy(shares, bother, ss.at[4], sr.at[4], other)

    a[...] = jnp.zeros_like(a)
    take_pivot(0)
    a[0] = info[0]

    def panel(k, carry):
        start = pl.multiple_of(k * 128, 128)
        rows = [a[k, 8 * g : 8 * g + 8, pl.ds(start, 128)] for g in range(16)]
        right = inverse_factor(rows)
        for g in range(16):
            linv[k, 8 * g : 8 * g + 8, :] = right[g]

        @pl.when(k == 0)
        def _():
            for t in (1, 2):
                share_pivot(t)
            for t in (1, 2):
                take_pivot(t)
            for i in range(1, 4):
                a[i, :, 128 * i : 512] = info[i, :, 128 * i : 512]

        @pl.when(k < 3)
        def _():
            w[k] = dot(linv[k], a[k], 1, 0)
            for i in range(1, 4):
                right_of = slice(128 * i, 512)
                a[i, :, right_of] = a[i, :, right_of] - dot(
                    w[k, :, 128 * i : 128 * i + 128], w[k, :, right_of], 0, 0
                )

        @pl.when(k == 1)
        def _():
            for j in range(2):
                for o in range(1, NY):
                    from_b1(j, o).wait_recv()
                both = bgot[0, j]
                for o in range(1, NY):
                    both = both + bgot[o, j]
                shares[32 * j : 32 * j + 32, :] = both
            swap_b().start()

        @pl.when(k == 2)
        def _():
            swap_b().wait()
            later = jnp.full((64, 512), s, jnp.int32) == 1
            shares[...] = shares[...] + jnp.where(later, bother[...], 0.0)
            for j in range(3):
                solve(j)
                eliminate(j)

        return carry

    lax.fori_loop(0, 4, panel, 0)
    solve(3)

    for wait in pending:
        wait()

    def finish(o, carry):
        q = (r + o) % NR
        pull(q).wait_recv()
        push(q).wait_send()
        return carry

    lax.fori_loop(1, NR, finish, 0)


def assemble_kernel(got, out):
    r, c = lax.axis_index("row"), lax.axis_index("col")
    row_ids = r * 16 + lax.broadcasted_iota(jnp.int32, (16, 128), 0)
    lanes = lax.broadcasted_iota(jnp.int32, (16, 128), 1)
    for l in range(16):
        cyc, half = l // 2, l % 2
        xs, y0, lane0 = cyc // 2, half * 4, cyc % 2 * 32
        both = jnp.concatenate([got[(y0 + q) * NX + xs, :, lane0 : lane0 + 32] for q in range(4)], axis=1)
        column_ids = (cyc * NZ + c) * 256 + half * 128 + lanes
        out[:, l, :] = jnp.where(column_ids >= row_ids, both, 0.0)


def on_device(prior_root, observations, live_rows):
    vmem = pl.BlockSpec(memory_space=pltpu.VMEM)
    hbm = pl.BlockSpec(memory_space=pltpu.HBM)

    def buf(*shape):
        return pltpu.VMEM(shape, F32)

    def dma(*shape):
        return pltpu.SemaphoreType.DMA(shape)

    got = pl.pallas_call(
        update_kernel,
        out_shape=jax.ShapeDtypeStruct((NR, 16, 64), F32),
        in_specs=[pl.BlockSpec(memory_space=pltpu.SMEM), hbm, hbm],
        out_specs=vmem,
        scratch_shapes=[
            buf(OBS, 16, 128), buf(OBS, 2, 128), buf(PRI, 16, 128), buf(8, ROWS, 256), buf(2, NX * ROWS, 256),
            buf(NX * ROWS, 512), buf(4, 128, 512), buf(3, NX, 32, 128), buf(3, 32, 128), buf(3, NY, 32, 128),
            buf(3, 32, 128), buf(3, 32, 128), buf(4, 128, 512),
            buf(2, 256, 512), buf(NY, 2, 32, 512), buf(64, 512), buf(64, 512),
            buf(4, 128, 512), buf(4, 128, 128), buf(4, 128, 512), buf(512, 64),
            dma(3), dma(4, CHUNKS), dma(2, CHUNKS), dma(2, NX - 1), dma(2, NX),
            dma(NX - 1, 2), dma(NX, 2), dma(3, NX - 1), dma(3, NX), dma(3, NY - 1), dma(3, NY), dma(5), dma(5),
            dma(3, NZ - 1), dma(3, NZ), dma(3, NX - 1), dma(3, NX), dma(2, NY - 1), dma(2, NY), dma(NR), dma(NR),
        ],
        compiler_params=pltpu.CompilerParams(
            collective_id=0, has_side_effects=True, vmem_limit_bytes=60 << 20
        ),
        name="update",
    )(live_rows, observations.reshape(OBS, 16, 128), prior_root.reshape(512, 16, 128))
    rows = pl.pallas_call(
        assemble_kernel,
        out_shape=jax.ShapeDtypeStruct((16, 16, 128), F32),
        in_specs=[vmem],
        out_specs=vmem,
        name="assemble",
    )(got)
    return rows.reshape(1, 16, 8, 1, 256)


def solution(mesh):
    placed = (
        P(None, None, "col", None),
        P("section", "row", None, "col", None),
        P("section", "row"),
    )
    return jax.shard_map(
        on_device,
        mesh=mesh,
        in_specs=placed,
        out_specs=P("section", "row", None, "col", None),
        check_vma=False,
    )
```
